256 devices in a mesh: exc: 16 (over y, z_hi), space: 16 (over z_lo, x, core).
Axes of the slice: x: 4, y: 4, z: 8 (z_hi: 4, z_lo: 2; z = z_hi * 2 + z_lo), core: 2. Of those that a mesh axis runs over, the one named last changes fastest.
Arguments:
- adj_e: float32 [16, 192, 4096], P('exc', None, 'space'), may hold values from -6 to 6
- adj_h: float32 [16, 192, 4096], P('exc', None, 'space'), may hold values from -6 to 6
- adj_j: float32 [16, 192, 4096], P('exc', None, 'space'), may hold values from -6 to 6
- fwd_e: bfloat16 [16, 5, 192, 4096], P('exc', None, None, 'space'), may hold values from -6 to 6
- inv_eps: float32 [64, 4096], P(None, 'space'), may hold values from 0.08 to 1
- drude_weight: float32 [64, 4096], P(None, 'space'), may hold values from 0.5 to 20
- neighbor: int32 [6, 4096], P(None, 'space'), may hold values from -1 to 4095, as said below
- design_map: int32 [4096], P('space'), may hold values from 0 to 2047, as said below
- port_elems: int32 [16, 2048], P('exc', 'space'), may hold values from 0 to 4095, as said below
- port_profile: float32 [16, 192, 2048], P('exc', None, 'space'), may hold values from -48 to 48
Outputs:
- adj_e_out: float32 [16, 192, 4096], P('exc', None, 'space')
- adj_h_out: float32 [16, 192, 4096], P('exc', None, 'space')
- grad_eps: float32 [64, 2048], P(None, ('space', 'exc'))
- grad_drude: float32 [64, 2048], P(None, ('space', 'exc'))
The draws below stay inside these ranges and needn't reach their ends.
Inputs may be any that keep to these rules, and one draw needn't show every extreme that they name: neighbor[f, e] is the element across face f (x-, x+, y-, y+, z-, z+) of element e, which touches it with its opposite face; it is -1 across the x- face of the first and the x+ face of the last element layer. Elements are stored layer by layer in layers of 128 elements along x, so each block of 256 elements is 2 whole layers; a y or z neighbour lies in the same layer (periodic in y and z), an x neighbour in the adjacent layer. `design_map`: an element of the b-th block of 256 elements maps to a pixel of the b-th block of 128 pixels, and every pixel holds exactly two elements. `port_elems`: columns b * 128 to (b + 1) * 128 - 1 of each row hold 128 distinct elements of the b-th block of 256 elements.
All inputs are finite; a program needn't handle non-finite values.
Results may differ from the reference program's by a relative error of at most 0.00035.
Values sent between devices are 32-bit elements; how exact they have to be, the bound alone decides.
A program may use at most 64 MiB of HBM per device.

```python
import math
import jax
import jax.numpy as jnp
import numpy as np
from jax import lax

NODES = 64
GY = 16
GZ = 8
LX_DEV = 2
STEPS = 4
NSRC_DEV = 128
ELEM_DEV = 256
ELEMS = 4096
PIX_DEV = 128
PIX = 2048
NSRC = 2048
EXC = 16
N_SPACE = 16


def draw_neighbor(key, part):
    total_layers = LX_DEV * N_SPACE
    cells = GY * GZ

    def one_layer(number):
        return jax.random.permutation(jax.random.fold_in(key, number), cells).astype(jnp.int32)
    orders = jax.vmap(one_layer)(jnp.arange(total_layers, dtype=jnp.int32))
    places = jnp.argsort(orders, axis=1).astype(jnp.int32)
    layer_ids = jnp.arange(total_layers, dtype=jnp.int32)[:, None]
    cell_y = orders // GZ
    cell_z = orders % GZ

    def in_layer(target_cells):
        return layer_ids * cells + jnp.take_along_axis(places, target_cells, axis=1)
    below = (layer_ids - 1) * cells + jnp.take_along_axis(jnp.roll(places, 1, axis=0), orders, axis=1)
    below = jnp.where(layer_ids == 0, -1, below)
    above = (layer_ids + 1) * cells + jnp.take_along_axis(jnp.roll(places, -1, axis=0), orders, axis=1)
    above = jnp.where(layer_ids == total_layers - 1, -1, above)
    y_minus = in_layer((cell_y - 1) % GY * GZ + cell_z)
    y_plus = in_layer((cell_y + 1) % GY * GZ + cell_z)
    z_minus = in_layer(cell_y * GZ + (cell_z - 1) % GZ)
    z_plus = in_layer(cell_y * GZ + (cell_z + 1) % GZ)
    return jnp.stack([below, above, y_minus, y_plus, z_minus, z_plus]).reshape(6, total_layers * cells).astype(jnp.int32)


def draw_design_map(key, part):

    def one_block(number):
        order = jax.random.permutation(jax.random.fold_in(key, number), ELEM_DEV).astype(jnp.int32)
        return order // 2 + number * PIX_DEV
    return jax.vmap(one_block)(jnp.arange(N_SPACE, dtype=jnp.int32)).reshape(N_SPACE * ELEM_DEV).astype(jnp.int32)


def draw_port_elems(key, part):

    def one_block(number):
        inner_key = jax.random.fold_in(key, number)
        middle = 1 + jax.random.permutation(inner_key, ELEM_DEV - 2).astype(jnp.int32)[:NSRC_DEV - 2]
        chosen = jnp.concatenate([jnp.array([0, ELEM_DEV - 1], jnp.int32), middle])
        order = jax.random.permutation(jax.random.fold_in(inner_key, 7), NSRC_DEV)
        return chosen[order] + number % N_SPACE * ELEM_DEV
    numbers = jnp.arange(EXC * N_SPACE, dtype=jnp.int32)
    return jax.vmap(one_block)(numbers).reshape(EXC, N_SPACE * NSRC_DEV).astype(jnp.int32)


def levels(own_key, dims, cuts, low, largest):
    gain = 1.0
    for axis_at, shards_of in cuts:
        heights = jax.random.uniform(jax.random.fold_in(jax.random.fold_in(own_key, 6), axis_at), (shards_of,), jnp.float32, low / len(cuts), largest / len(cuts))
        gain = gain * jnp.repeat(jnp.exp(heights), dims[axis_at] // shards_of).reshape((-1,) + (1,) * (len(dims) - 1 - axis_at))
    return gain


def scatter_about(rng, extent, deviation, bound, shards=(), kind=jnp.bfloat16):
    values = deviation * jax.random.normal(rng, extent, jnp.float32)
    if shards:
        values = values * levels(rng, extent, shards, -0.22, 0.18)
    return jnp.clip(values, -bound, bound).astype(kind)


def setup_inputs(seed: int = 0) -> dict:
    keys = jax.random.split(jax.random.key(seed), 11)
    return {
        "adj_e": scatter_about(keys[0], (EXC, 3 * NODES, ELEMS), 1.0, 6.0, ((0, 16), (2, 16)), jnp.float32),
        "adj_h": scatter_about(keys[1], (EXC, 3 * NODES, ELEMS), 1.0, 6.0, ((0, 16), (2, 16)), jnp.float32),
        "adj_j": scatter_about(keys[2], (EXC, 3 * NODES, ELEMS), 1.0, 6.0, ((0, 16), (2, 16)), jnp.float32),
        "fwd_e": scatter_about(keys[3], (EXC, STEPS + 1, 3 * NODES, ELEMS), 1.0, 6.0, ((0, 16), (3, 16))),
        "inv_eps": jnp.clip(0.08 + 0.92 * jax.random.uniform(keys[4], (NODES, ELEMS), jnp.float32) ** levels(keys[4], (NODES, ELEMS), ((1, 16),), -0.2, 0.2), 0.08, 1.0),
        "drude_weight": jnp.clip(jnp.exp(math.log(20.0) - 3.6888795 * jax.random.uniform(keys[5], (NODES, ELEMS), jnp.float32) ** levels(keys[5], (NODES, ELEMS), ((1, 16),), -0.2, 0.2)), 0.5, 20.0),
        "neighbor": draw_neighbor(jax.random.fold_in(keys[10], 71), 0),
        "design_map": draw_design_map(jax.random.fold_in(keys[10], 71), 0),
        "port_elems": draw_port_elems(jax.random.fold_in(keys[10], 71), 0),
        "port_profile": scatter_about(keys[9], (EXC, 3 * NODES, NSRC), 8.0, 48.0, ((0, 16), (2, 16)), jnp.float32),
    }


TIME_STEP = 0.025
DAMPING = 0.5

def node_tables():
    points = np.array([-1.0, -1.0 / np.sqrt(5.0), 1.0 / np.sqrt(5.0), 1.0])
    barycentric = np.array([1.0 / np.prod([points[j] - points[k] for k in range(4) if k != j]) for j in range(4)])
    deriv = np.zeros((4, 4))
    for row in range(4):
        for column in range(4):
            if row != column:
                deriv[row, column] = barycentric[column] / barycentric[row] / (points[row] - points[column])
        deriv[row, row] = -np.sum(deriv[row])
    identity = np.eye(4)
    along_x = 2.0 * np.kron(np.kron(deriv, identity), identity)
    along_y = 2.0 * np.kron(np.kron(identity, deriv), identity)
    along_z = 2.0 * np.kron(np.kron(identity, identity), deriv)
    curl_table = np.zeros((192, 192))
    curl_table[0:64, 64:128] = -along_z
    curl_table[0:64, 128:192] = along_y
    curl_table[64:128, 0:64] = along_z
    curl_table[64:128, 128:192] = -along_x
    curl_table[128:192, 0:64] = -along_y
    curl_table[128:192, 64:128] = along_x
    numbers = np.arange(64).reshape(4, 4, 4)
    faces = np.stack([numbers[0].ravel(), numbers[3].ravel(), numbers[:, 0].ravel(), numbers[:, 3].ravel(), numbers[:, :, 0].ravel(), numbers[:, :, 3].ravel()])
    lift_table = np.zeros((192, 288))
    for face in range(6):
        direction = face // 2
        sign = 1.0 if face % 2 else -1.0
        for component in range(3):
            for other in range(3):
                parity = (component - direction) * (direction - other) * (other - component) / 2.0
                if parity != 0:
                    for node in range(16):
                        lift_table[component * 64 + faces[face, node], other * 96 + face * 16 + node] += 6.0 * sign * parity
    return (curl_table, faces, lift_table)

def flux_term(field, neighbor, faces, lift_table):
    count = field.shape[1]
    cube = field.reshape(3, 64, count)
    inner = cube[:, faces.reshape(-1), :].reshape(288, count)
    pieces = []
    for face in range(6):
        rows = cube[:, faces[face ^ 1], :]
        target = neighbor[face]
        picked = jnp.take(rows, jnp.clip(target, 0, count - 1), axis=2)
        pieces.append(picked * (target >= 0).astype(jnp.float32))
    outer = jnp.stack(pieces, axis=1).reshape(288, count)
    return jnp.dot(lift_table, inner - outer, preferred_element_type=jnp.float32, precision=lax.Precision.HIGHEST)

def reference(adj_e, adj_h, adj_j, fwd_e, inv_eps, drude_weight, neighbor, design_map, port_elems, port_profile):
    curl_np, faces, lift_np = node_tables()
    curl_table = jnp.asarray(curl_np, jnp.float32)
    lift_table = jnp.asarray(lift_np, jnp.float32)
    inverse = jnp.tile(inv_eps, (3, 1))
    plasma = jnp.tile(drude_weight, (3, 1))
    count = adj_e.shape[2]

    def one_excitation(carry, inputs):
        electric, magnetic, current, history, ports, profile = inputs
        source = jnp.zeros((3 * NODES, count), jnp.float32).at[:, ports].add(profile)
        sens_eps = jnp.zeros((NODES, count), jnp.float32)
        sens_drude = jnp.zeros((NODES, count), jnp.float32)
        for step in range(STEPS):
            magnetic = magnetic + TIME_STEP * (flux_term(electric, neighbor, faces, lift_table) - jnp.dot(curl_table, electric, preferred_element_type=jnp.float32, precision=lax.Precision.HIGHEST))
            current = (1.0 - TIME_STEP * DAMPING) * current + TIME_STEP * plasma * electric
            electric = electric + TIME_STEP * inverse * (jnp.dot(curl_table, magnetic, preferred_element_type=jnp.float32, precision=lax.Precision.HIGHEST) - flux_term(magnetic, neighbor, faces, lift_table) - current - source)
            before = history[step].astype(jnp.float32)
            change = history[step + 1].astype(jnp.float32) - before
            sens_eps = sens_eps + lax.optimization_barrier(jnp.sum((electric * change).reshape(3, NODES, count), axis=0))
            sens_drude = sens_drude + lax.optimization_barrier(jnp.sum((current * before).reshape(3, NODES, count), axis=0))
        return ((carry[0] + sens_eps, carry[1] + sens_drude), (electric, magnetic))
    start = (jnp.zeros((NODES, count), jnp.float32), jnp.zeros((NODES, count), jnp.float32))
    (total_eps, total_drude), (out_e, out_h) = lax.scan(one_excitation, start, (adj_e, adj_h, adj_j, fwd_e, port_elems, port_profile))
    excitations = adj_e.shape[0]
    grad_eps = jax.ops.segment_sum(total_eps.T, design_map, num_segments=PIX).T / excitations
    grad_drude = jax.ops.segment_sum(total_drude.T, design_map, num_segments=PIX).T / excitations
    return (out_e, out_h, grad_eps, grad_drude)
```

```python
import functools

import jax
import jax.numpy as jnp
import ml_dtypes
import numpy as np
from jax import lax
from jax.experimental import pallas as pl
from jax.experimental.pallas import tpu as pltpu
from jax.sharding import PartitionSpec as P

STEPS = 4
LAYER = 128
TIME_STEP = 0.025
DAMPING = 0.5
GAIN = 6.0 * TIME_STEP
MESH = pl.DeviceIdType.MESH


def operator_table():
    points = np.array([-1.0, -1.0 / np.sqrt(5.0), 1.0 / np.sqrt(5.0), 1.0])
    barycentric = np.array(
        [1.0 / np.prod([points[j] - points[k] for k in range(4) if k != j]) for j in range(4)]
    )
    deriv = np.zeros((4, 4))
    for row in range(4):
        for column in range(4):
            if row != column:
                deriv[row, column] = (
                    barycentric[column] / barycentric[row] / (points[row] - points[column])
                )
        deriv[row, row] = -np.sum(deriv[row])
    identity = np.eye(4)
    along_x = 2.0 * np.kron(np.kron(deriv, identity), identity)
    along_y = 2.0 * np.kron(np.kron(identity, deriv), identity)
    along_z = 2.0 * np.kron(np.kron(identity, identity), deriv)
    curl = np.zeros((192, 192))
    curl[0:64, 64:128] = -along_z
    curl[0:64, 128:192] = along_y
    curl[64:128, 0:64] = along_z
    curl[64:128, 128:192] = -along_x
    curl[128:192, 0:64] = -along_y
    curl[128:192, 64:128] = along_x
    numbers = np.arange(64).reshape(4, 4, 4)
    faces = [
        numbers[0].ravel(),
        numbers[3].ravel(),
        numbers[:, 0].ravel(),
        numbers[:, 3].ravel(),
        numbers[:, :, 0].ravel(),
        numbers[:, :, 3].ravel(),
    ]
    inner = np.zeros((192, 192))
    for face in range(6):
        direction = face // 2
        sign = 1.0 if face % 2 else -1.0
        for component in range(3):
            for other in range(3):
                parity = (component - direction) * (direction - other) * (other - component) / 2.0
                for node in faces[face]:
                    inner[component * 64 + node, other * 64 + node] += sign * parity
    return inner - curl / 6.0


def split_table():
    table = operator_table()
    high = table.astype(ml_dtypes.bfloat16)
    low = (table - high.astype(np.float64)).astype(ml_dtypes.bfloat16)
    return np.concatenate([high, low], axis=0)


def halves(value):
    high = value.astype(jnp.bfloat16)
    low = (value - high.astype(jnp.float32)).astype(jnp.bfloat16)
    return high, low


def pick(value, index):
    index = jnp.broadcast_to(index, value.shape)
    return jnp.take_along_axis(value, index, axis=1, mode="promise_in_bounds")


def rows_of(ref, layer, start):
    return jnp.concatenate(
        [ref[layer, 64 + start : 80 + start], ref[layer, 128 + start : 144 + start]], axis=0
    )


def kernel(
    n_exc,
    n_space,
    adj_e,
    adj_h,
    adj_j,
    fwd_e,
    inv_eps,
    drude,
    neighbor,
    design,
    ports,
    profile,
    table,
    out_e,
    out_h,
    out_eps,
    out_drude,
    e_ref,
    h_ref,
    j_ref,
    s_ref,
    g_ref,
    f_ref,
    v_ref,
    w_ref,
    nb_ref,
    dm_ref,
    pe_ref,
    pp_ref,
    tb_ref,
    send_e,
    send_h,
    recv_e,
    recv_h,
    sums,
    parts,
    load_sem,
    send_sem,
    recv_sem,
    part_send_sem,
    part_recv_sem,
    store_sem,
):
    me_exc = lax.axis_index("exc")
    me_space = lax.axis_index("space")
    left = lax.rem(me_space + n_space - 1, n_space)
    right = lax.rem(me_space + 1, n_space)
    own_rows = LAYER // n_exc

    loads = []

    def load(src, dst):
        copy = pltpu.make_async_copy(src, dst, load_sem.at[len(loads)])
        copy.start()
        loads.append(copy)
        return copy

    def load_layers(src, dst):
        return [load(src.at[..., pl.ds(n * LAYER, LAYER)], dst.at[n]) for n in range(2)]

    got_nb = load(neighbor, nb_ref)
    got_e = load_layers(adj_e.at[0], e_ref)
    got_tb = load(table, tb_ref)
    got_h = load_layers(adj_h.at[0], h_ref)
    got_w = load_layers(drude, w_ref)
    got_v = load_layers(inv_eps, v_ref)
    got_j = load_layers(adj_j.at[0], j_ref)
    got_pe = load(ports, pe_ref)
    got_pp = load(profile.at[0], pp_ref)
    got_f = load_layers(fwd_e.at[0], f_ref)
    got_dm = load(design, dm_ref)

    barrier = pltpu.get_barrier_semaphore()
    for peer in (left, right):
        pl.semaphore_signal(barrier, inc=1, device_id={"space": peer}, device_id_type=MESH)
    for hop in range(1, n_exc):
        peer = lax.rem(me_exc + hop, n_exc)
        pl.semaphore_signal(barrier, inc=1, device_id={"exc": peer}, device_id_type=MESH)

    sublane = lax.broadcasted_iota(jnp.int32, (8, LAYER), 0)
    lower = sublane < 4

    got_nb.wait()
    table_nb = nb_ref[...]
    place = table_nb & (LAYER - 1)

    def face(number, layer):
        return place[number : number + 1, layer * LAYER : (layer + 1) * LAYER]

    def inside(number, layer):
        cut = table_nb[number : number + 1, layer * LAYER : (layer + 1) * LAYER]
        return (cut >= 0).astype(jnp.float32)

    along_y = [jnp.where(lower, face(3, n), face(2, n)) for n in range(2)]
    along_y = [jnp.concatenate([index] * 8, axis=0) for index in along_y]
    low_z = [face(4, n) for n in range(2)]
    high_z = [face(5, n) for n in range(2)]
    between = [face(1, 0), face(0, 1)]
    beyond = [face(0, 0), face(1, 1)]
    exists = [inside(0, 0), inside(1, 1)]

    def fill_local(field_ref):
        field = jnp.concatenate([field_ref[0], field_ref[1]], axis=1)
        high, low = halves(field)
        whole = jnp.dot(tb_ref[...], high, preferred_element_type=jnp.float32)
        rest = jnp.dot(tb_ref[0:192, :], low, preferred_element_type=jnp.float32)
        total = whole[0:192] + (whole[192:384] + rest)
        zeros = jnp.zeros((48, LAYER), jnp.float32)
        for n in range(2):
            own = field_ref[n].reshape(3, 4, 2, 8, LAYER)
            edge = jnp.concatenate(
                [
                    jnp.where(lower, own[0, :, 0], own[0, :, 1]),
                    jnp.where(lower, own[2, :, 0], own[2, :, 1]),
                ],
                axis=0,
            )
            outer = pick(edge.reshape(64, LAYER), along_y[n]).reshape(8, 8, LAYER)
            outer = pltpu.roll(outer, 4, 1)
            zero = jnp.zeros((4, 8, LAYER), jnp.float32)
            o_x, o_z = outer[0:4], outer[4:8]
            to_x = jnp.stack([jnp.where(lower, o_z, zero), jnp.where(lower, zero, -o_z)], axis=1)
            to_z = jnp.stack([jnp.where(lower, -o_x, zero), jnp.where(lower, zero, o_x)], axis=1)
            if n == 0:
                side = pick(rows_of(field_ref, 1, 0), between[0])
                to_y = jnp.concatenate([zeros, side[16:32]], axis=0)
                to_z2 = jnp.concatenate([zeros, -side[0:16]], axis=0)
            else:
                side = pick(rows_of(field_ref, 0, 48), between[1])
                to_y = jnp.concatenate([-side[16:32], zeros], axis=0)
                to_z2 = jnp.concatenate([side[0:16], zeros], axis=0)
            mine = total[:, n * LAYER : (n + 1) * LAYER]
            g_ref[n, 0:64] = mine[0:64] + to_x.reshape(64, LAYER)
            g_ref[n, 64:128] = mine[64:128] + to_y
            g_ref[n, 128:192] = mine[128:192] + to_z.reshape(64, LAYER) + to_z2
            far = pick(field_ref[n, pl.ds(0, 32, stride=4), :], high_z[n])
            g_ref[n, pl.ds(3, 32, stride=4), :] += jnp.concatenate(
                [far[16:32], -far[0:16]], axis=0
            )
            near = pick(field_ref[n, pl.ds(3, 32, stride=4), :], low_z[n])
            g_ref[n, pl.ds(0, 32, stride=4), :] += jnp.concatenate(
                [-near[16:32], near[0:16]], axis=0
            )

    def exchange(step, kind, src, dst):
        copies = []
        for side, peer in ((0, left), (1, right)):
            copy = pltpu.make_async_remote_copy(
                src_ref=src.at[step, side],
                dst_ref=dst.at[step, 1 - side],
                send_sem=send_sem.at[step, kind, side],
                recv_sem=recv_sem.at[step, kind, 1 - side],
                device_id={"space": peer},
                device_id_type=MESH,
            )
            copy.start()
            copies.append(copy)
        return copies

    sens = [[jnp.zeros((64, LAYER), jnp.float32)] * 2 for _ in range(2)]

    def add_eps(step):
        for n in range(2):
            change = f_ref[n, step + 1].astype(jnp.float32) - f_ref[n, step].astype(jnp.float32)
            product = (e_ref[n] * change).reshape(3, 64, LAYER)
            sens[0][n] = sens[0][n] + (product[0] + product[1] + product[2])

    for copy in got_e:
        copy.wait()

    for step in range(STEPS):
        send_e[step, 0] = rows_of(e_ref, 0, 0)
        send_e[step, 1] = rows_of(e_ref, 1, 48)
        if step == 0:
            pl.semaphore_wait(barrier, 2 + n_exc - 1)
        e_copies = exchange(step, 0, send_e, recv_e)

        if step == 0:
            got_tb.wait()
        fill_local(e_ref)
        if step == 0:
            for copy in got_h:
                copy.wait()
        for n in range(2):
            h_ref[n] = h_ref[n] + GAIN * g_ref[n]
        send_h[step, 0] = rows_of(h_ref, 0, 0)
        send_h[step, 1] = rows_of(h_ref, 1, 48)
        h_copies = exchange(step, 1, send_h, recv_h)

        if step == 0:
            for copy in got_w + got_v + got_j + [got_pe, got_pp]:
                copy.wait()
            element = lax.broadcasted_iota(jnp.int32, (2 * LAYER, LAYER), 0)
            chosen = ((pe_ref[...] & (2 * LAYER - 1)) == element).astype(jnp.bfloat16)
            high, low = halves(pp_ref[...])
            contract = (((1,), (1,)), ((), ()))
            source = lax.dot_general(
                high, chosen, contract, preferred_element_type=jnp.float32
            ) + lax.dot_general(low, chosen, contract, preferred_element_type=jnp.float32)
            for n in range(2):
                s_ref[n] = source[:, n * LAYER : (n + 1) * LAYER]
            for copy in got_f:
                copy.wait()
        else:
            add_eps(step - 1)
        for n in range(2):
            current = j_ref[n].reshape(3, 64, LAYER)
            electric = e_ref[n].reshape(3, 64, LAYER)
            current = (1.0 - TIME_STEP * DAMPING) * current + (TIME_STEP * w_ref[n]) * electric
            j_ref[n] = current.reshape(192, LAYER)
            before = f_ref[n, step].astype(jnp.float32).reshape(3, 64, LAYER)
            product = current * before
            sens[1][n] = sens[1][n] + (product[0] + product[1] + product[2])
            drive = (TIME_STEP * v_ref[n]) * (current + s_ref[n].reshape(3, 64, LAYER))
            e_ref[n] = (electric - drive).reshape(192, LAYER)

        for copy in e_copies:
            copy.wait_recv()
        outer = pick(recv_e[step, 0], beyond[0]) * (GAIN * exists[0])
        h_ref[0, 64:80] += -outer[16:32]
        h_ref[0, 128:144] += outer[0:16]
        outer = pick(recv_e[step, 1], beyond[1]) * (GAIN * exists[1])
        h_ref[1, 112:128] += outer[16:32]
        h_ref[1, 176:192] += -outer[0:16]

        fill_local(h_ref)
        if step == STEPS - 1:
            stores = [
                pltpu.make_async_copy(
                    h_ref.at[n], out_h.at[0, :, pl.ds(n * LAYER, LAYER)], store_sem.at[n]
                )
                for n in range(2)
            ]
            for copy in stores:
                copy.start()

        for n in range(2):
            kick = (GAIN * v_ref[n]) * g_ref[n].reshape(3, 64, LAYER)
            e_ref[n] = e_ref[n] - kick.reshape(192, LAYER)
        for copy in h_copies:
            copy.wait_recv()
        outer = pick(recv_h[step, 0], beyond[0])
        own = GAIN * send_e[step, 0]
        speed = (GAIN * v_ref[0, 0:16]) * exists[0]
        e_ref[0, 64:80] += speed * (outer[16:32] - own[0:16])
        e_ref[0, 128:144] += -speed * (outer[0:16] + own[16:32])
        outer = pick(recv_h[step, 1], beyond[1])
        own = GAIN * send_e[step, 1]
        speed = (GAIN * v_ref[1, 48:64]) * exists[1]
        e_ref[1, 112:128] += -speed * (outer[16:32] + own[0:16])
        e_ref[1, 176:192] += speed * (outer[0:16] - own[16:32])
        for copy in e_copies + h_copies:
            copy.wait_send()

    for n in range(2):
        copy = pltpu.make_async_copy(
            e_ref.at[n], out_e.at[0, :, pl.ds(n * LAYER, LAYER)], store_sem.at[2 + n]
        )
        copy.start()
        stores.append(copy)
    add_eps(STEPS - 1)
    got_dm.wait()
    pixel = lax.broadcasted_iota(jnp.int32, (LAYER, 2 * LAYER), 0)
    members = ((dm_ref[...] & (LAYER - 1)) == pixel).astype(jnp.bfloat16)
    stacked = jnp.concatenate(
        [jnp.concatenate(sens[0], axis=1), jnp.concatenate(sens[1], axis=1)], axis=0
    )
    high, low = halves(stacked)
    contract = (((1,), (1,)), ((), ()))
    sums[...] = lax.dot_general(
        members, high, contract, preferred_element_type=jnp.float32
    ) + lax.dot_general(members, low, contract, preferred_element_type=jnp.float32)
    part_copies = []
    for hop in range(1, n_exc):
        peer = lax.rem(me_exc + hop, n_exc)
        start = pl.multiple_of(peer * own_rows, own_rows)
        copy = pltpu.make_async_remote_copy(
            src_ref=sums.at[pl.ds(start, own_rows)],
            dst_ref=parts.at[hop],
            send_sem=part_send_sem.at[hop],
            recv_sem=part_recv_sem.at[hop],
            device_id={"exc": peer},
            device_id_type=MESH,
        )
        copy.start()
        part_copies.append(copy)
    total = sums[pl.ds(pl.multiple_of(me_exc * own_rows, own_rows), own_rows)]
    for hop in range(1, n_exc):
        part_copies[hop - 1].wait_recv()
        total = total + parts[hop]
    total = total * (1.0 / n_exc)
    out_eps[...] = total[:, 0:64]
    out_drude[...] = total[:, 64:128]
    for copy in part_copies:
        copy.wait_send()
    for copy in stores:
        copy.wait()


def local(n_exc, n_space, *args):
    (adj_e, adj_h, adj_j, fwd_e, inv_eps, drude, neighbor, design, ports, profile) = args
    own_rows = LAYER // n_exc
    f32 = jnp.float32
    anywhere = pl.BlockSpec(memory_space=pltpu.HBM)
    in_vmem = pl.BlockSpec(memory_space=pltpu.VMEM)
    new_e, new_h, grad_eps, grad_drude = pl.pallas_call(
        functools.partial(kernel, n_exc, n_space),
        out_shape=(
            jax.ShapeDtypeStruct(adj_e.shape, f32),
            jax.ShapeDtypeStruct(adj_h.shape, f32),
            jax.ShapeDtypeStruct((own_rows, 64), f32),
            jax.ShapeDtypeStruct((own_rows, 64), f32),
        ),
        in_specs=[anywhere] * 11,
        out_specs=(anywhere, anywhere, in_vmem, in_vmem),
        scratch_shapes=[
            pltpu.VMEM((2, 192, LAYER), f32),
            pltpu.VMEM((2, 192, LAYER), f32),
            pltpu.VMEM((2, 192, LAYER), f32),
            pltpu.VMEM((2, 192, LAYER), f32),
            pltpu.VMEM((2, 192, LAYER), f32),
            pltpu.VMEM((2, STEPS + 1, 192, LAYER), jnp.bfloat16),
            pltpu.VMEM((2, 64, LAYER), f32),
            pltpu.VMEM((2, 64, LAYER), f32),
            pltpu.VMEM((6, 2 * LAYER), jnp.int32),
            pltpu.VMEM((1, 2 * LAYER), jnp.int32),
            pltpu.VMEM((1, LAYER), jnp.int32),
            pltpu.VMEM((192, LAYER), f32),
            pltpu.VMEM((384, 192), jnp.bfloat16),
            pltpu.VMEM((STEPS, 2, 32, LAYER), f32),
            pltpu.VMEM((STEPS, 2, 32, LAYER), f32),
            pltpu.VMEM((STEPS, 2, 32, LAYER), f32),
            pltpu.VMEM((STEPS, 2, 32, LAYER), f32),
            pltpu.VMEM((LAYER, LAYER), f32),
            pltpu.VMEM((n_exc, own_rows, LAYER), f32),
            pltpu.SemaphoreType.DMA((20,)),
            pltpu.SemaphoreType.DMA((STEPS, 2, 2)),
            pltpu.SemaphoreType.DMA((STEPS, 2, 2)),
            pltpu.SemaphoreType.DMA((n_exc,)),
            pltpu.SemaphoreType.DMA((n_exc,)),
            pltpu.SemaphoreType.DMA((4,)),
        ],
        compiler_params=pltpu.CompilerParams(
            collective_id=0, has_side_effects=True, vmem_limit_bytes=60 << 20
        ),
        name="adjoint_steps",
    )(
        adj_e,
        adj_h,
        adj_j,
        fwd_e,
        inv_eps,
        drude,
        neighbor,
        design.reshape(1, 2 * LAYER),
        ports,
        profile,
        jnp.asarray(split_table()),
    )
    return new_e, new_h, grad_eps.T, grad_drude.T


def solution(mesh):
    return jax.shard_map(
        functools.partial(local, mesh.shape["exc"], mesh.shape["space"]),
        mesh=mesh,
        in_specs=(
            P("exc", None, "space"),
            P("exc", None, "space"),
            P("exc", None, "space"),
            P("exc", None, None, "space"),
            P(None, "space"),
            P(None, "space"),
            P(None, "space"),
            P("space"),
            P("exc", "space"),
            P("exc", None, "space"),
        ),
        out_specs=(
            P("exc", None, "space"),
            P("exc", None, "space"),
            P(None, ("space", "exc")),
            P(None, ("space", "exc")),
        ),
        check_vma=False,
    )
```

```python
import functools

import jax
import jax.numpy as jnp
import ml_dtypes
import numpy as np
from jax import lax
from jax.experimental import pallas as pl
from jax.experimental.pallas import tpu as pltpu
from jax.sharding import PartitionSpec as P

STEPS = 4
LAYER = 128
TIME_STEP = 0.025
DAMPING = 0.5
GAIN = 6.0 * TIME_STEP
MESH = pl.DeviceIdType.MESH


def operator_table():
    points = np.array([-1.0, -1.0 / np.sqrt(5.0), 1.0 / np.sqrt(5.0), 1.0])
    barycentric = np.array(
        [1.0 / np.prod([points[j] - points[k] for k in range(4) if k != j]) for j in range(4)]
    )
    deriv = np.zeros((4, 4))
    for row in range(4):
        for column in range(4):
            if row != column:
                deriv[row, column] = (
                    barycentric[column] / barycentric[row] / (points[row] - points[column])
                )
        deriv[row, row] = -np.sum(deriv[row])
    identity = np.eye(4)
    along_x = 2.0 * np.kron(np.kron(deriv, identity), identity)
    along_y = 2.0 * np.kron(np.kron(identity, deriv), identity)
    along_z = 2.0 * np.kron(np.kron(identity, identity), deriv)
    curl = np.zeros((192, 192))
    curl[0:64, 64:128] = -along_z
    curl[0:64, 128:192] = along_y
    curl[64:128, 0:64] = along_z
    curl[64:128, 128:192] = -along_x
    curl[128:192, 0:64] = -along_y
    curl[128:192, 64:128] = along_x
    numbers = np.arange(64).reshape(4, 4, 4)
    faces = [
        numbers[0].ravel(),
        numbers[3].ravel(),
        numbers[:, 0].ravel(),
        numbers[:, 3].ravel(),
        numbers[:, :, 0].ravel(),
        numbers[:, :, 3].ravel(),
    ]
    inner = np.zeros((192, 192))
    for face in range(6):
        direction = face // 2
        sign = 1.0 if face % 2 else -1.0
        for component in range(3):
            for other in range(3):
                parity = (component - direction) * (direction - other) * (other - component) / 2.0
                for node in faces[face]:
                    inner[component * 64 + node, other * 64 + node] += sign * parity
    return inner - curl / 6.0


def split_table():
    table = operator_table()
    high = table.astype(ml_dtypes.bfloat16)
    low = (table - high.astype(np.float64)).astype(ml_dtypes.bfloat16)
    return np.concatenate([high, low], axis=0)


def halves(value):
    high = value.astype(jnp.bfloat16)
    low = (value - high.astype(jnp.float32)).astype(jnp.bfloat16)
    return high, low


def pick(value, index):
    index = jnp.broadcast_to(index, value.shape)
    return jnp.take_along_axis(value, index, axis=1, mode="promise_in_bounds")


def rows_of(ref, layer, start):
    return jnp.concatenate(
        [ref[layer, 64 + start : 80 + start], ref[layer, 128 + start : 144 + start]], axis=0
    )


def kernel(
    n_exc,
    n_space,
    adj_e,
    adj_h,
    adj_j,
    fwd_e,
    inv_eps,
    drude,
    neighbor,
    design,
    ports,
    profile,
    table,
    out_e,
    out_h,
    out_eps,
    out_drude,
    e_ref,
    h_ref,
    j_ref,
    s_ref,
    g_ref,
    f_ref,
    v_ref,
    w_ref,
    nb_ref,
    dm_ref,
    pe_ref,
    pp_ref,
    tb_ref,
    send_e,
    send_h,
    recv_e,
    recv_h,
    sums,
    parts,
    load_sem,
    send_sem,
    recv_sem,
    part_send_sem,
    part_recv_sem,
    store_sem,
):
    me_exc = lax.axis_index("exc")
    me_space = lax.axis_index("space")
    left = lax.rem(me_space + n_space - 1, n_space)
    right = lax.rem(me_space + 1, n_space)
    own_rows = LAYER // n_exc

    loads = []

    def load(src, dst):
        copy = pltpu.make_async_copy(src, dst, load_sem.at[len(loads)])
        copy.start()
        loads.append(copy)
        return copy

    def load_layers(src, dst):
        return [load(src.at[..., pl.ds(n * LAYER, LAYER)], dst.at[n]) for n in range(2)]

    got_nb = load(neighbor, nb_ref)
    got_e = load_layers(adj_e.at[0], e_ref)
    got_tb = load(table, tb_ref)
    got_h = load_layers(adj_h.at[0], h_ref)
    got_w = load_layers(drude, w_ref)
    got_v = load_layers(inv_eps, v_ref)
    got_j = load_layers(adj_j.at[0], j_ref)
    got_pe = load(ports, pe_ref)
    got_pp = load(profile.at[0], pp_ref)
    got_f = load_layers(fwd_e.at[0], f_ref)
    got_dm = load(design, dm_ref)

    barrier = pltpu.get_barrier_semaphore()
    for peer in (left, right):
        pl.semaphore_signal(barrier, inc=1, device_id={"space": peer}, device_id_type=MESH)
    for hop in range(1, n_exc):
        peer = lax.rem(me_exc + hop, n_exc)
        pl.semaphore_signal(barrier, inc=1, device_id={"exc": peer}, device_id_type=MESH)

    sublane = lax.broadcasted_iota(jnp.int32, (8, LAYER), 0)
    lower = sublane < 4

    got_nb.wait()
    table_nb = nb_ref[...]
    place = table_nb & (LAYER - 1)

    def face(number, layer):
        return place[number : number + 1, layer * LAYER : (layer + 1) * LAYER]

    def inside(number, layer):
        cut = table_nb[number : number + 1, layer * LAYER : (layer + 1) * LAYER]
        return (cut >= 0).astype(jnp.float32)

    along_y = [jnp.where(lower, face(3, n), face(2, n)) for n in range(2)]
    along_y = [jnp.concatenate([index] * 8, axis=0) for index in along_y]
    low_z = [face(4, n) for n in range(2)]
    high_z = [face(5, n) for n in range(2)]
    between = [face(1, 0), face(0, 1)]
    beyond = [face(0, 0), face(1, 1)]
    exists = [inside(0, 0), inside(1, 1)]

    def fill_local(field_ref):
        field = jnp.concatenate([field_ref[0], field_ref[1]], axis=1)
        high, low = halves(field)
        whole = jnp.dot(tb_ref[...], high, preferred_element_type=jnp.float32)
        rest = jnp.dot(tb_ref[0:192, :], low, preferred_element_type=jnp.float32)
        total = whole[0:192] + (whole[192:384] + rest)
        zeros = jnp.zeros((48, LAYER), jnp.float32)
        for n in range(2):
            own = field_ref[n].reshape(3, 4, 2, 8, LAYER)
            edge = jnp.concatenate(
                [
                    jnp.where(lower, own[0, :, 0], own[0, :, 1]),
                    jnp.where(lower, own[2, :, 0], own[2, :, 1]),
                ],
                axis=0,
            )
            outer = pick(edge.reshape(64, LAYER), along_y[n]).reshape(8, 8, LAYER)
            outer = pltpu.roll(outer, 4, 1)
            zero = jnp.zeros((4, 8, LAYER), jnp.float32)
            o_x, o_z = outer[0:4], outer[4:8]
            to_x = jnp.stack([jnp.where(lower, o_z, zero), jnp.where(lower, zero, -o_z)], axis=1)
            to_z = jnp.stack([jnp.where(lower, -o_x, zero), jnp.where(lower, zero, o_x)], axis=1)
            if n == 0:
                side = pick(rows_of(field_ref, 1, 0), between[0])
                to_y = jnp.concatenate([zeros, side[16:32]], axis=0)
                to_z2 = jnp.concatenate([zeros, -side[0:16]], axis=0)
            else:
                side = pick(rows_of(field_ref, 0, 48), between[1])
                to_y = jnp.concatenate([-side[16:32], zeros], axis=0)
                to_z2 = jnp.concatenate([side[0:16], zeros], axis=0)
            mine = total[:, n * LAYER : (n + 1) * LAYER]
            g_ref[n, 0:64] = mine[0:64] + to_x.reshape(64, LAYER)
            g_ref[n, 64:128] = mine[64:128] + to_y
            g_ref[n, 128:192] = mine[128:192] + to_z.reshape(64, LAYER) + to_z2
            far = pick(field_ref[n, pl.ds(0, 32, stride=4), :], high_z[n])
            g_ref[n, pl.ds(3, 32, stride=4), :] += jnp.concatenate(
                [far[16:32], -far[0:16]], axis=0
            )
            near = pick(field_ref[n, pl.ds(3, 32, stride=4), :], low_z[n])
            g_ref[n, pl.ds(0, 32, stride=4), :] += jnp.concatenate(
                [-near[16:32], near[0:16]], axis=0
            )

    def exchange(step, kind, src, dst):
        copies = []
        for side, peer in ((0, left), (1, right)):
            copy = pltpu.make_async_remote_copy(
                src_ref=src.at[step, side],
                dst_ref=dst.at[step, 1 - side],
                send_sem=send_sem.at[step, kind, side],
                recv_sem=recv_sem.at[step, kind, 1 - side],
                device_id={"space": peer},
                device_id_type=MESH,
            )
            copy.start()
            copies.append(copy)
        return copies

    sens = [[jnp.zeros((64, LAYER), jnp.float32)] * 2 for _ in range(2)]

    def add_eps(step):
        for n in range(2):
            change = f_ref[n, step + 1].astype(jnp.float32) - f_ref[n, step].astype(jnp.float32)
            product = (e_ref[n] * change).reshape(3, 64, LAYER)
            sens[0][n] = sens[0][n] + (product[0] + product[1] + product[2])

    for copy in got_e:
        copy.wait()

    for step in range(STEPS):
        send_e[step, 0] = rows_of(e_ref, 0, 0)
        send_e[step, 1] = rows_of(e_ref, 1, 48)
        if step == 0:
            pl.semaphore_wait(barrier, 2 + n_exc - 1)
        e_copies = exchange(step, 0, send_e, recv_e)

        if step == 0:
            got_tb.wait()
        fill_local(e_ref)
        if step == 0:
            for copy in got_h:
                copy.wait()
        for n in range(2):
            h_ref[n] = h_ref[n] + GAIN * g_ref[n]
        send_h[step, 0] = rows_of(h_ref, 0, 0)
        send_h[step, 1] = rows_of(h_ref, 1, 48)
        h_copies = exchange(step, 1, send_h, recv_h)

        if step == 0:
            for copy in got_w + got_v + got_j + [got_pe, got_pp]:
                copy.wait()
            element = lax.broadcasted_iota(jnp.int32, (2 * LAYER, LAYER), 0)
            chosen = ((pe_ref[...] & (2 * LAYER - 1)) == element).astype(jnp.bfloat16)
            high, low = halves(pp_ref[...])
            contract = (((1,), (1,)), ((), ()))
            source = lax.dot_general(
                high, chosen, contract, preferred_element_type=jnp.float32
            ) + lax.dot_general(low, chosen, contract, preferred_element_type=jnp.float32)
            for n in range(2):
                s_ref[n] = source[:, n * LAYER : (n + 1) * LAYER]
            for copy in got_f:
                copy.wait()
        else:
            add_eps(step - 1)
        for n in range(2):
            current = j_ref[n].reshape(3, 64, LAYER)
            electric = e_ref[n].reshape(3, 64, LAYER)
            current = (1.0 - TIME_STEP * DAMPING) * current + (TIME_STEP * w_ref[n]) * electric
            j_ref[n] = current.reshape(192, LAYER)
            before = f_ref[n, step].astype(jnp.float32).reshape(3, 64, LAYER)
            product = current * before
            sens[1][n] = sens[1][n] + (product[0] + product[1] + product[2])
            drive = (TIME_STEP * v_ref[n]) * (current + s_ref[n].reshape(3, 64, LAYER))
            e_ref[n] = (electric - drive).reshape(192, LAYER)

        for copy in e_copies:
            copy.wait_recv()
        outer = pick(recv_e[step, 0], beyond[0]) * (GAIN * exists[0])
        h_ref[0, 64:80] += -outer[16:32]
        h_ref[0, 128:144] += outer[0:16]
        outer = pick(recv_e[step, 1], beyond[1]) * (GAIN * exists[1])
        h_ref[1, 112:128] += outer[16:32]
        h_ref[1, 176:192] += -outer[0:16]

        fill_local(h_ref)
        if step == STEPS - 1:
            stores = [
                pltpu.make_async_copy(
                    h_ref.at[n], out_h.at[0, :, pl.ds(n * LAYER, LAYER)], store_sem.at[n]
                )
                for n in range(2)
            ]
            for copy in stores:
                copy.start()

        for n in range(2):
            kick = (GAIN * v_ref[n]) * g_ref[n].reshape(3, 64, LAYER)
            e_ref[n] = e_ref[n] - kick.reshape(192, LAYER)
        for copy in h_copies:
            copy.wait_recv()
        outer = pick(recv_h[step, 0], beyond[0])
        own = GAIN * send_e[step, 0]
        speed = (GAIN * v_ref[0, 0:16]) * exists[0]
        e_ref[0, 64:80] += speed * (outer[16:32] - own[0:16])
        e_ref[0, 128:144] += -speed * (outer[0:16] + own[16:32])
        outer = pick(recv_h[step, 1], beyond[1])
        own = GAIN * send_e[step, 1]
        speed = (GAIN * v_ref[1, 48:64]) * exists[1]
        e_ref[1, 112:128] += -speed * (outer[16:32] + own[0:16])
        e_ref[1, 176:192] += speed * (outer[0:16] - own[16:32])
        for copy in e_copies + h_copies:
            copy.wait_send()

    for n in range(2):
        copy = pltpu.make_async_copy(
            e_ref.at[n], out_e.at[0, :, pl.ds(n * LAYER, LAYER)], store_sem.at[2 + n]
        )
        copy.start()
        stores.append(copy)
    add_eps(STEPS - 1)
    got_dm.wait()
    pixel = lax.broadcasted_iota(jnp.int32, (LAYER, 2 * LAYER), 0)
    members = ((dm_ref[...] & (LAYER - 1)) == pixel).astype(jnp.bfloat16)
    stacked = jnp.concatenate(
        [jnp.concatenate(sens[0], axis=1), jnp.concatenate(sens[1], axis=1)], axis=0
    )
    high, low = halves(stacked)
    contract = (((1,), (1,)), ((), ()))
    sums[...] = lax.dot_general(
        members, high, contract, preferred_element_type=jnp.float32
    ) + lax.dot_general(members, low, contract, preferred_element_type=jnp.float32)
    part_copies = []
    for hop in range(1, n_exc):
        peer = lax.rem(me_exc + hop, n_exc)
        start = pl.multiple_of(peer * own_rows, own_rows)
        copy = pltpu.make_async_remote_copy(
            src_ref=sums.at[pl.ds(start, own_rows)],
            dst_ref=parts.at[hop],
            send_sem=part_send_sem.at[hop],
            recv_sem=part_recv_sem.at[hop],
            device_id={"exc": peer},
            device_id_type=MESH,
        )
        copy.start()
        part_copies.append(copy)
    total = sums[pl.ds(pl.multiple_of(me_exc * own_rows, own_rows), own_rows)]
    for hop in range(1, n_exc):
        part_copies[hop - 1].wait_recv()
        total = total + parts[hop]
    total = total * (1.0 / n_exc)
    out_eps[...] = total[:, 0:64]
    out_drude[...] = total[:, 64:128]
    for copy in part_copies:
        copy.wait_send()
    for copy in stores:
        copy.wait()


def write_kernel(e_in, h_in, a_in, b_in, e_out, h_out, a_out, b_out, sem):
    copies = [
        pltpu.make_async_copy(src, dst, sem.at[at])
        for at, (src, dst) in enumerate(
            ((e_in, e_out), (h_in, h_out), (a_in, a_out), (b_in, b_out))
        )
    ]
    for copy in copies:
        copy.start()
    for copy in copies:
        copy.wait()


def write(*arrays):
    spec = pl.BlockSpec(memory_space=pltpu.HBM)
    return pl.pallas_call(
        write_kernel,
        out_shape=tuple(jax.ShapeDtypeStruct(a.shape, a.dtype) for a in arrays),
        in_specs=[pl.BlockSpec(memory_space=pltpu.VMEM)] * 4,
        out_specs=(spec,) * 4,
        scratch_shapes=[pltpu.SemaphoreType.DMA((4,))],
        compiler_params=pltpu.CompilerParams(vmem_limit_bytes=2 << 20),
        name="write_out",
    )(*arrays)


def local(n_exc, n_space, *args):
    (adj_e, adj_h, adj_j, fwd_e, inv_eps, drude, neighbor, design, ports, profile) = args
    own_rows = LAYER // n_exc
    f32 = jnp.float32
    anywhere = pl.BlockSpec(memory_space=pltpu.HBM)
    in_vmem = pl.BlockSpec(memory_space=pltpu.VMEM)
    new_e, new_h, grad_eps, grad_drude = pl.pallas_call(
        functools.partial(kernel, n_exc, n_space),
        out_shape=(
            jax.ShapeDtypeStruct(adj_e.shape, f32),
            jax.ShapeDtypeStruct(adj_h.shape, f32),
            jax.ShapeDtypeStruct((own_rows, 64), f32),
            jax.ShapeDtypeStruct((own_rows, 64), f32),
        ),
        in_specs=[anywhere] * 11,
        out_specs=(anywhere, anywhere, in_vmem, in_vmem),
        scratch_shapes=[
            pltpu.VMEM((2, 192, LAYER), f32),
            pltpu.VMEM((2, 192, LAYER), f32),
            pltpu.VMEM((2, 192, LAYER), f32),
            pltpu.VMEM((2, 192, LAYER), f32),
            pltpu.VMEM((2, 192, LAYER), f32),
            pltpu.VMEM((2, STEPS + 1, 192, LAYER), jnp.bfloat16),
            pltpu.VMEM((2, 64, LAYER), f32),
            pltpu.VMEM((2, 64, LAYER), f32),
            pltpu.VMEM((6, 2 * LAYER), jnp.int32),
            pltpu.VMEM((1, 2 * LAYER), jnp.int32),
            pltpu.VMEM((1, LAYER), jnp.int32),
            pltpu.VMEM((192, LAYER), f32),
            pltpu.VMEM((384, 192), jnp.bfloat16),
            pltpu.VMEM((STEPS, 2, 32, LAYER), f32),
            pltpu.VMEM((STEPS, 2, 32, LAYER), f32),
            pltpu.VMEM((STEPS, 2, 32, LAYER), f32),
            pltpu.VMEM((STEPS, 2, 32, LAYER), f32),
            pltpu.VMEM((LAYER, LAYER), f32),
            pltpu.VMEM((n_exc, own_rows, LAYER), f32),
            pltpu.SemaphoreType.DMA((20,)),
            pltpu.SemaphoreType.DMA((STEPS, 2, 2)),
            pltpu.SemaphoreType.DMA((STEPS, 2, 2)),
            pltpu.SemaphoreType.DMA((n_exc,)),
            pltpu.SemaphoreType.DMA((n_exc,)),
            pltpu.SemaphoreType.DMA((4,)),
        ],
        compiler_params=pltpu.CompilerParams(
            collective_id=0, has_side_effects=True, vmem_limit_bytes=16 << 20
        ),
        name="adjoint_steps",
    )(
        *[pltpu.with_memory_space_constraint(x, pltpu.HBM) for x in (adj_e, adj_h, adj_j, fwd_e, inv_eps, drude, neighbor, design.reshape(1, 2 * LAYER), ports, profile, jnp.asarray(split_table()))]
    )
    new_e, new_h, grad_eps, grad_drude = write(new_e, new_h, grad_eps, grad_drude)
    return new_e, new_h, grad_eps.T, grad_drude.T


def solution(mesh):
    return jax.shard_map(
        functools.partial(local, mesh.shape["exc"], mesh.shape["space"]),
        mesh=mesh,
        in_specs=(
            P("exc", None, "space"),
            P("exc", None, "space"),
            P("exc", None, "space"),
            P("exc", None, None, "space"),
            P(None, "space"),
            P(None, "space"),
            P(None, "space"),
            P("space"),
            P("exc", "space"),
            P("exc", None, "space"),
        ),
        out_specs=(
            P("exc", None, "space"),
            P("exc", None, "space"),
            P(None, ("space", "exc")),
            P(None, ("space", "exc")),
        ),
        check_vma=False,
    )
```

```python
import functools

import jax
import jax.numpy as jnp
import ml_dtypes
import numpy as np
from jax import lax
from jax.experimental import pallas as pl
from jax.experimental.pallas import tpu as pltpu
from jax.sharding import PartitionSpec as P

STEPS = 4
LAYER = 128
TIME_STEP = 0.025
DAMPING = 0.5
GAIN = 6.0 * TIME_STEP
MESH = pl.DeviceIdType.MESH


def operator_table():
    points = np.array([-1.0, -1.0 / np.sqrt(5.0), 1.0 / np.sqrt(5.0), 1.0])
    barycentric = np.array(
        [1.0 / np.prod([points[j] - points[k] for k in range(4) if k != j]) for j in range(4)]
    )
    deriv = np.zeros((4, 4))
    for row in range(4):
        for column in range(4):
            if row != column:
                deriv[row, column] = (
                    barycentric[column] / barycentric[row] / (points[row] - points[column])
                )
        deriv[row, row] = -np.sum(deriv[row])
    identity = np.eye(4)
    along_x = 2.0 * np.kron(np.kron(deriv, identity), identity)
    along_y = 2.0 * np.kron(np.kron(identity, deriv), identity)
    along_z = 2.0 * np.kron(np.kron(identity, identity), deriv)
    curl = np.zeros((192, 192))
    curl[0:64, 64:128] = -along_z
    curl[0:64, 128:192] = along_y
    curl[64:128, 0:64] = along_z
    curl[64:128, 128:192] = -along_x
    curl[128:192, 0:64] = -along_y
    curl[128:192, 64:128] = along_x
    numbers = np.arange(64).reshape(4, 4, 4)
    faces = [
        numbers[0].ravel(),
        numbers[3].ravel(),
        numbers[:, 0].ravel(),
        numbers[:, 3].ravel(),
        numbers[:, :, 0].ravel(),
        numbers[:, :, 3].ravel(),
    ]
    inner = np.zeros((192, 192))
    for face in range(6):
        direction = face // 2
        sign = 1.0 if face % 2 else -1.0
        for component in range(3):
            for other in range(3):
                parity = (component - direction) * (direction - other) * (other - component) / 2.0
                for node in faces[face]:
                    inner[component * 64 + node, other * 64 + node] += sign * parity
    return inner - curl / 6.0


def split_table():
    table = operator_table()
    high = table.astype(ml_dtypes.bfloat16)
    low = (table - high.astype(np.float64)).astype(ml_dtypes.bfloat16)
    return np.concatenate([high, low], axis=0)


def split_faces():
    table = split_table()
    tables = []
    for start in (0, 48):
        rows = np.concatenate([np.arange(64, 80), np.arange(128, 144)]) + start
        high, low = table[0:192, rows], table[192:384, rows]
        tables.append(np.concatenate([high, low, high], axis=1))
    return np.stack(tables)


def halves(value):
    high = value.astype(jnp.bfloat16)
    low = (value - high.astype(jnp.float32)).astype(jnp.bfloat16)
    return high, low


def pick(value, index):
    index = jnp.broadcast_to(index, value.shape)
    return jnp.take_along_axis(value, index, axis=1, mode="promise_in_bounds")


def rows_of(ref, layer, start):
    return jnp.concatenate(
        [ref[layer, 64 + start : 80 + start], ref[layer, 128 + start : 144 + start]], axis=0
    )


def turn(trace, sign):
    return jnp.concatenate([sign * trace[16:32], -sign * trace[0:16]], axis=0)


def add_rows(ref, layer, start, value):
    ref[layer, 64 + start : 80 + start] += value[0:16]
    ref[layer, 128 + start : 144 + start] += value[16:32]


MINE = (0, 48)
THEIRS = (48, 0)
SIGN = (-1.0, 1.0)


def kernel(
    n_exc,
    n_space,
    adj_e,
    adj_h,
    adj_j,
    fwd_e,
    inv_eps,
    drude,
    neighbor,
    design,
    ports,
    profile,
    table,
    face_table,
    out_e,
    out_h,
    out_eps,
    out_drude,
    e_ref,
    h_ref,
    j_ref,
    s_ref,
    g_ref,
    de_ref,
    f_ref,
    v_ref,
    w_ref,
    kick_ref,
    nb_ref,
    dm_ref,
    pe_ref,
    pp_ref,
    tb_ref,
    fb_ref,
    send_t,
    recv_t,
    recv_v,
    recv_nb,
    sums,
    parts,
    load_sem,
    send_sem,
    recv_sem,
    once_send_sem,
    once_recv_sem,
    part_send_sem,
    part_recv_sem,
    store_sem,
):
    me_exc = lax.axis_index("exc")
    me_space = lax.axis_index("space")
    left = lax.rem(me_space + n_space - 1, n_space)
    right = lax.rem(me_space + 1, n_space)
    own_rows = LAYER // n_exc
    f32 = jnp.float32

    barrier = pltpu.get_barrier_semaphore()
    for peer in (left, right):
        pl.semaphore_signal(barrier, inc=1, device_id={"space": peer}, device_id_type=MESH)
    for hop in range(1, n_exc):
        peer = lax.rem(me_exc + hop, n_exc)
        pl.semaphore_signal(barrier, inc=1, device_id={"exc": peer}, device_id_type=MESH)

    loads = []

    def load(src, dst):
        copy = pltpu.make_async_copy(src, dst, load_sem.at[len(loads)])
        copy.start()
        loads.append(copy)
        return copy

    def load_layers(src, dst):
        return [load(src.at[..., pl.ds(n * LAYER, LAYER)], dst.at[n]) for n in range(2)]

    got_nb = load(neighbor, nb_ref)
    got_e = load_layers(adj_e.at[0], e_ref)
    got_tb = load(table, tb_ref)
    got_h = load_layers(adj_h.at[0], h_ref)
    got_v = load_layers(inv_eps, v_ref)
    got_w = load_layers(drude, w_ref)
    got_j = load_layers(adj_j.at[0], j_ref)
    got_pe = load(ports, pe_ref)
    got_pp = load(profile.at[0], pp_ref)
    got_fb = load(face_table, fb_ref)
    got_f = load_layers(fwd_e.at[0], f_ref)
    got_dm = load(design, dm_ref)

    sublane = lax.broadcasted_iota(jnp.int32, (8, LAYER), 0)
    lower = sublane < 4
    first_k = (sublane & 3) == 0
    last_k = (sublane & 3) == 3

    got_nb.wait()
    table_nb = nb_ref[...]
    place = table_nb & (LAYER - 1)

    def face(number, layer):
        return place[number : number + 1, layer * LAYER : (layer + 1) * LAYER]

    def inside(number, layer):
        cut = table_nb[number : number + 1, layer * LAYER : (layer + 1) * LAYER]
        return (cut >= 0).astype(f32)

    edge_y = [jnp.where(lower, face(3, n), face(2, n)) for n in range(2)]
    edge_z = [jnp.where(first_k, face(5, n), face(4, n)) for n in range(2)]
    along_y = [jnp.concatenate([index] * 8, axis=0) for index in edge_y]
    low_z = [face(4, n) for n in range(2)]
    high_z = [face(5, n) for n in range(2)]
    between = [face(1, 0), face(0, 1)]
    beyond = [face(0, 0), face(1, 1)]
    exists = [inside(0, 0), inside(1, 1)]

    def product(field):
        high, low = halves(field)
        whole = jnp.dot(tb_ref[...], high, preferred_element_type=f32)
        rest = jnp.dot(tb_ref[0:192, :], low, preferred_element_type=f32)
        return whole[0:192] + (whole[192:384] + rest)

    def fill_local(field_ref):
        total = product(jnp.concatenate([field_ref[0], field_ref[1]], axis=1))
        zeros = jnp.zeros((48, LAYER), f32)
        for n in range(2):
            own = field_ref[n].reshape(3, 4, 2, 8, LAYER)
            edge = jnp.concatenate(
                [
                    jnp.where(lower, own[0, :, 0], own[0, :, 1]),
                    jnp.where(lower, own[2, :, 0], own[2, :, 1]),
                ],
                axis=0,
            )
            outer = pick(edge.reshape(64, LAYER), along_y[n]).reshape(8, 8, LAYER)
            outer = pltpu.roll(outer, 4, 1)
            zero = jnp.zeros((4, 8, LAYER), f32)
            o_x, o_z = outer[0:4], outer[4:8]
            to_x = jnp.stack([jnp.where(lower, o_z, zero), jnp.where(lower, zero, -o_z)], axis=1)
            to_z = jnp.stack([jnp.where(lower, -o_x, zero), jnp.where(lower, zero, o_x)], axis=1)
            if n == 0:
                side = turn(pick(rows_of(field_ref, 1, 0), between[0]), 1.0)
                to_y = jnp.concatenate([zeros, side[0:16]], axis=0)
                to_z2 = jnp.concatenate([zeros, side[16:32]], axis=0)
            else:
                side = turn(pick(rows_of(field_ref, 0, 48), between[1]), -1.0)
                to_y = jnp.concatenate([side[0:16], zeros], axis=0)
                to_z2 = jnp.concatenate([side[16:32], zeros], axis=0)
            mine = total[:, n * LAYER : (n + 1) * LAYER]
            g_ref[n, 0:64] = mine[0:64] + to_x.reshape(64, LAYER)
            g_ref[n, 64:128] = mine[64:128] + to_y
            g_ref[n, 128:192] = mine[128:192] + to_z.reshape(64, LAYER) + to_z2
            far = pick(field_ref[n, pl.ds(0, 32, stride=4), :], high_z[n])
            g_ref[n, pl.ds(3, 32, stride=4), :] += jnp.concatenate(
                [far[16:32], -far[0:16]], axis=0
            )
            near = pick(field_ref[n, pl.ds(3, 32, stride=4), :], low_z[n])
            g_ref[n, pl.ds(0, 32, stride=4), :] += jnp.concatenate(
                [-near[16:32], near[0:16]], axis=0
            )

    def from_y(rows, index):
        outer = pltpu.roll(pick(jnp.where(lower, rows[0:8], rows[8:16]), index), 4, 0)
        zero = jnp.zeros((8, LAYER), f32)
        return jnp.concatenate(
            [jnp.where(lower, outer, zero), jnp.where(lower, zero, -outer)], axis=0
        )

    def from_z(rows, index):
        parts_z = []
        zero = jnp.zeros((8, LAYER), f32)
        for half in (rows[0:8], rows[8:16]):
            outer = pick(half, index)
            parts_z.append(
                jnp.where(last_k, pltpu.roll(outer, 3, 0), zero)
                - jnp.where(first_k, pltpu.roll(outer, 5, 0), zero)
            )
        return jnp.concatenate(parts_z, axis=0)

    def remote(src, dst, sems, side):
        copy = pltpu.make_async_remote_copy(
            src_ref=src,
            dst_ref=dst,
            send_sem=sems[0],
            recv_sem=sems[1],
            device_id={"space": (left, right)[side]},
            device_id_type=MESH,
        )
        copy.start()
        return copy

    sent = []

    def send_trace(window, kind, ref):
        copies = []
        for side in range(2):
            send_t[window, kind, side] = rows_of(ref, side, MINE[side])
            copies.append(
                remote(
                    send_t.at[window, kind, side],
                    recv_t.at[window, kind, 1 - side],
                    (send_sem.at[window, kind, side], recv_sem.at[window, kind, 1 - side]),
                    side,
                )
            )
        sent.extend(copies)
        return copies

    sens = [[jnp.zeros((64, LAYER), f32)] * 2 for _ in range(2)]

    def add_eps(step):
        for n in range(2):
            change = f_ref[n, step + 1].astype(f32) - f_ref[n, step].astype(f32)
            term = (e_ref[n] * change).reshape(3, 64, LAYER)
            sens[0][n] = sens[0][n] + (term[0] + term[1] + term[2])

    def drive(step):
        for n in range(2):
            electric = e_ref[n].reshape(3, 64, LAYER)
            current = (1.0 - TIME_STEP * DAMPING) * j_ref[n].reshape(3, 64, LAYER)
            current = current + (TIME_STEP * w_ref[n]) * electric
            j_ref[n] = current.reshape(192, LAYER)
            term = current * f_ref[n, step].astype(f32).reshape(3, 64, LAYER)
            sens[1][n] = sens[1][n] + (term[0] + term[1] + term[2])
            push = (TIME_STEP * v_ref[n]) * (current + s_ref[n].reshape(3, 64, LAYER))
            e_ref[n] = (electric - push).reshape(192, LAYER)

    def kick(n):
        return (kick_ref[n] * g_ref[n].reshape(3, 64, LAYER)).reshape(192, LAYER)

    pl.semaphore_wait(barrier, 2 + n_exc - 1)
    once = []
    for side in range(2):
        lanes = pl.ds(side * LAYER, LAYER)
        for at, (src, dst) in enumerate(((inv_eps, recv_v), (neighbor, recv_nb))):
            once.append(
                remote(
                    src.at[:, lanes],
                    dst.at[1 - side],
                    (once_send_sem.at[at, side], once_recv_sem.at[at, 1 - side]),
                    side,
                )
            )
    ghost_y, ghost_z = [None, None], [None, None]

    for copy in got_e:
        copy.wait()

    for window in range(STEPS // 2):
        step = 2 * window
        e0 = send_trace(window, 0, e_ref)
        if window == 0:
            got_tb.wait()
        fill_local(e_ref)
        if window == 0:
            for copy in got_h:
                copy.wait()
        for n in range(2):
            h_ref[n] = h_ref[n] + GAIN * g_ref[n]
        h1 = send_trace(window, 1, h_ref)

        if window == 0:
            for copy in got_w + got_v + got_j + got_f + [got_pe, got_pp, got_fb]:
                copy.wait()
            element = lax.broadcasted_iota(jnp.int32, (2 * LAYER, LAYER), 0)
            chosen = ((pe_ref[...] & (2 * LAYER - 1)) == element).astype(jnp.bfloat16)
            high, low = halves(pp_ref[...])
            contract = (((1,), (1,)), ((), ()))
            source = lax.dot_general(
                high, chosen, contract, preferred_element_type=f32
            ) + lax.dot_general(low, chosen, contract, preferred_element_type=f32)
            for n in range(2):
                s_ref[n] = source[:, n * LAYER : (n + 1) * LAYER]
                kick_ref[n] = GAIN * v_ref[n]
        drive(step)
        fill_local(h_ref)
        for n in range(2):
            e_ref[n] = e_ref[n] - kick(n)
        e1 = send_trace(window, 2, e_ref)
        fill_local(e_ref)
        for n in range(2):
            h_ref[n] = h_ref[n] + GAIN * g_ref[n]
        h2 = send_trace(window, 3, h_ref)

        if window == 0:
            for copy in once:
                copy.wait_recv()
            for side in range(2):
                kick_ref[2 + side] = GAIN * pick(recv_v[side], beyond[side])
                far = recv_nb[side] & (LAYER - 1)
                back = jnp.broadcast_to(far[1 - side : 2 - side], (8, LAYER))

                def through(number):
                    rows = jnp.broadcast_to(far[number : number + 1], (8, LAYER))
                    return pick(back, pick(rows, beyond[side]))

                ghost_y[side] = jnp.where(lower, through(3), through(2))
                ghost_z[side] = jnp.where(first_k, through(5), through(4))

        for copy in e0 + h1:
            copy.wait_recv()
        mine_dh, their_dh, their_h = [], [], []
        for side in range(2):
            sign = SIGN[side]
            outer = pick(recv_t[window, 0, side], beyond[side]) * exists[side]
            mine_dh.append(turn(outer, GAIN * sign))
            their_dh.append(turn(send_t[window, 0, side], -GAIN * sign))
            their_h.append(
                (pick(recv_t[window, 1, side], beyond[side]) + their_dh[side]) * exists[side]
            )
        pairs = ((mine_dh[0], their_dh[1]), (mine_dh[1], their_dh[0]))
        spread = []
        for at in range(2):
            high, low = halves(jnp.concatenate(pairs[at], axis=1))
            spread.append(
                jnp.dot(
                    fb_ref[at],
                    jnp.concatenate([high, high, low], axis=0),
                    preferred_element_type=f32,
                )
            )
        for side in range(2):
            for ghost in range(2):
                layer = 2 + side if ghost else side
                start = THEIRS[side] if ghost else MINE[side]
                change = their_dh[side] if ghost else mine_dh[side]
                index_y = ghost_y[side] if ghost else edge_y[side]
                index_z = ghost_z[side] if ghost else edge_z[side]
                if ghost:
                    across = send_t[window, 1, side] + mine_dh[side]
                    across = turn(across, -SIGN[side])
                    out = spread[1 - side][:, LAYER : 2 * LAYER]
                else:
                    across = turn(their_h[side], SIGN[side])
                    out = spread[side][:, 0:LAYER]
                edge = from_y(change[16:32], index_y) + from_z(change[0:16], index_z)

                def with_face(rows, extra):
                    end = start + 16
                    middle = rows[start:end] + extra
                    if start == 0:
                        return jnp.concatenate([middle, rows[end:64]], axis=0)
                    return jnp.concatenate([rows[0:start], middle], axis=0)

                speed = kick_ref[layer]
                de_ref[layer, 0:64] = -speed * with_face(out[0:64], edge)
                de_ref[layer, 64:128] = -speed * with_face(out[64:128], across[0:16])
                de_ref[layer, 128:192] = -speed * with_face(out[128:192], across[16:32])
        for n in range(2):
            e_ref[n] = e_ref[n] + de_ref[n]
            add_rows(h_ref, n, MINE[n], mine_dh[n])

        high, low = halves(jnp.concatenate([de_ref[2], de_ref[3]], axis=1))
        cuts = [tb_ref[at : at + 16, :] for at in (112, 176, 64, 128)]
        lows = [tb_ref[192 + at : 208 + at, :] for at in (112, 176, 64, 128)]
        whole = jnp.dot(jnp.concatenate(cuts + lows, axis=0), high, preferred_element_type=f32)
        rest = jnp.dot(jnp.concatenate(cuts, axis=0), low, preferred_element_type=f32)
        near = whole[0:64] + (whole[64:128] + rest)
        their_dh2 = []
        for side in range(2):
            start = THEIRS[side]
            own = de_ref[2 + side, start : start + 16]
            edge = jnp.concatenate(
                [-from_z(own, ghost_z[side]), -from_y(own, ghost_y[side])], axis=0
            )
            across = turn(rows_of(e_ref, side, MINE[side]), -SIGN[side])
            lanes = slice(side * LAYER, (side + 1) * LAYER)
            at = slice(32 * side, 32 * side + 32)
            their_dh2.append(their_dh[side] + GAIN * (near[at, lanes] + edge + across))

        fill_local(de_ref)
        for n in range(2):
            h_ref[n] = h_ref[n] + GAIN * g_ref[n]
        for copy in e1:
            copy.wait_recv()
        for side in range(2):
            outer = pick(recv_t[window, 2, side], beyond[side])
            outer = (outer + rows_of(de_ref, 2 + side, THEIRS[side])) * exists[side]
            add_rows(h_ref, side, MINE[side], turn(outer, GAIN * SIGN[side]))
        if step + 2 == STEPS:
            stores = []
            for n in range(2):
                lanes = pl.ds(n * LAYER, LAYER)
                copy = pltpu.make_async_copy(h_ref.at[n], out_h.at[0, :, lanes], store_sem.at[n])
                copy.start()
                stores.append(copy)

        add_eps(step)
        drive(step + 1)
        fill_local(h_ref)
        for n in range(2):
            e_ref[n] = e_ref[n] - kick(n)
        for copy in h2:
            copy.wait_recv()
        for side in range(2):
            outer = pick(recv_t[window, 3, side], beyond[side])
            outer = turn((outer + their_dh2[side]) * exists[side], -SIGN[side])
            speed = kick_ref[side, MINE[side] : MINE[side] + 16]
            add_rows(
                e_ref,
                side,
                MINE[side],
                jnp.concatenate([speed * outer[0:16], speed * outer[16:32]], axis=0),
            )
        if step + 2 < STEPS:
            add_eps(step + 1)

    for n in range(2):
        lanes = pl.ds(n * LAYER, LAYER)
        copy = pltpu.make_async_copy(e_ref.at[n], out_e.at[0, :, lanes], store_sem.at[2 + n])
        copy.start()
        stores.append(copy)
    add_eps(STEPS - 1)
    got_dm.wait()
    pixel = lax.broadcasted_iota(jnp.int32, (LAYER, 2 * LAYER), 0)
    members = ((dm_ref[...] & (LAYER - 1)) == pixel).astype(jnp.bfloat16)
    stacked = jnp.concatenate(
        [jnp.concatenate(sens[0], axis=1), jnp.concatenate(sens[1], axis=1)], axis=0
    )
    high, low = halves(stacked)
    contract = (((1,), (1,)), ((), ()))
    sums[...] = lax.dot_general(
        members, high, contract, preferred_element_type=f32
    ) + lax.dot_general(members, low, contract, preferred_element_type=f32)
    part_copies = []
    for hop in range(1, n_exc):
        peer = lax.rem(me_exc + hop, n_exc)
        start = pl.multiple_of(peer * own_rows, own_rows)
        copy = pltpu.make_async_remote_copy(
            src_ref=sums.at[pl.ds(start, own_rows)],
            dst_ref=parts.at[hop],
            send_sem=part_send_sem.at[hop],
            recv_sem=part_recv_sem.at[hop],
            device_id={"exc": peer},
            device_id_type=MESH,
        )
        copy.start()
        part_copies.append(copy)
    for copy in sent + once:
        copy.wait_send()
    total = sums[pl.ds(pl.multiple_of(me_exc * own_rows, own_rows), own_rows)]
    for hop in range(1, n_exc):
        part_copies[hop - 1].wait_recv()
        total = total + parts[hop]
    total = total * (1.0 / n_exc)
    out_eps[...] = total[:, 0:64]
    out_drude[...] = total[:, 64:128]
    for copy in part_copies:
        copy.wait_send()
    for copy in stores:
        copy.wait()


def write_kernel(e_in, h_in, a_in, b_in, e_out, h_out, a_out, b_out, sem):
    copies = [
        pltpu.make_async_copy(src, dst, sem.at[at])
        for at, (src, dst) in enumerate(
            ((e_in, e_out), (h_in, h_out), (a_in, a_out), (b_in, b_out))
        )
    ]
    for copy in copies:
        copy.start()
    for copy in copies:
        copy.wait()


def write(*arrays):
    spec = pl.BlockSpec(memory_space=pltpu.HBM)
    return pl.pallas_call(
        write_kernel,
        out_shape=tuple(jax.ShapeDtypeStruct(a.shape, a.dtype) for a in arrays),
        in_specs=[pl.BlockSpec(memory_space=pltpu.VMEM)] * 4,
        out_specs=(spec,) * 4,
        scratch_shapes=[pltpu.SemaphoreType.DMA((4,))],
        compiler_params=pltpu.CompilerParams(vmem_limit_bytes=2 << 20),
        name="write_out",
    )(*arrays)


def local(n_exc, n_space, *args):
    (adj_e, adj_h, adj_j, fwd_e, inv_eps, drude, neighbor, design, ports, profile) = args
    own_rows = LAYER // n_exc
    f32 = jnp.float32
    anywhere = pl.BlockSpec(memory_space=pltpu.HBM)
    in_vmem = pl.BlockSpec(memory_space=pltpu.VMEM)
    new_e, new_h, grad_eps, grad_drude = pl.pallas_call(
        functools.partial(kernel, n_exc, n_space),
        out_shape=(
            jax.ShapeDtypeStruct(adj_e.shape, f32),
            jax.ShapeDtypeStruct(adj_h.shape, f32),
            jax.ShapeDtypeStruct((own_rows, 64), f32),
            jax.ShapeDtypeStruct((own_rows, 64), f32),
        ),
        in_specs=[anywhere] * 12,
        out_specs=(anywhere, anywhere, in_vmem, in_vmem),
        scratch_shapes=[
            pltpu.VMEM((2, 192, LAYER), f32),
            pltpu.VMEM((2, 192, LAYER), f32),
            pltpu.VMEM((2, 192, LAYER), f32),
            pltpu.VMEM((2, 192, LAYER), f32),
            pltpu.VMEM((2, 192, LAYER), f32),
            pltpu.VMEM((4, 192, LAYER), f32),
            pltpu.VMEM((2, STEPS + 1, 192, LAYER), jnp.bfloat16),
            pltpu.VMEM((2, 64, LAYER), f32),
            pltpu.VMEM((2, 64, LAYER), f32),
            pltpu.VMEM((4, 64, LAYER), f32),
            pltpu.VMEM((6, 2 * LAYER), jnp.int32),
            pltpu.VMEM((1, 2 * LAYER), jnp.int32),
            pltpu.VMEM((1, LAYER), jnp.int32),
            pltpu.VMEM((192, LAYER), f32),
            pltpu.VMEM((384, 192), jnp.bfloat16),
            pltpu.VMEM((2, 192, 96), jnp.bfloat16),
            pltpu.VMEM((STEPS // 2, 4, 2, 32, LAYER), f32),
            pltpu.VMEM((STEPS // 2, 4, 2, 32, LAYER), f32),
            pltpu.VMEM((2, 64, LAYER), f32),
            pltpu.VMEM((2, 6, LAYER), jnp.int32),
            pltpu.VMEM((LAYER, LAYER), f32),
            pltpu.VMEM((n_exc, own_rows, LAYER), f32),
            pltpu.SemaphoreType.DMA((24,)),
            pltpu.SemaphoreType.DMA((STEPS // 2, 4, 2)),
            pltpu.SemaphoreType.DMA((STEPS // 2, 4, 2)),
            pltpu.SemaphoreType.DMA((2, 2)),
            pltpu.SemaphoreType.DMA((2, 2)),
            pltpu.SemaphoreType.DMA((n_exc,)),
            pltpu.SemaphoreType.DMA((n_exc,)),
            pltpu.SemaphoreType.DMA((4,)),
        ],
        compiler_params=pltpu.CompilerParams(
            collective_id=0, has_side_effects=True, vmem_limit_bytes=16 << 20
        ),
        name="adjoint_steps",
    )(
        *[pltpu.with_memory_space_constraint(x, pltpu.HBM) for x in (adj_e, adj_h, adj_j, fwd_e, inv_eps, drude, neighbor, design.reshape(1, 2 * LAYER), ports, profile, jnp.asarray(split_table()), jnp.asarray(split_faces()))]
    )
    new_e, new_h, grad_eps, grad_drude = write(new_e, new_h, grad_eps, grad_drude)
    return new_e, new_h, grad_eps.T, grad_drude.T


def solution(mesh):
    return jax.shard_map(
        functools.partial(local, mesh.shape["exc"], mesh.shape["space"]),
        mesh=mesh,
        in_specs=(
            P("exc", None, "space"),
            P("exc", None, "space"),
            P("exc", None, "space"),
            P("exc", None, None, "space"),
            P(None, "space"),
            P(None, "space"),
            P(None, "space"),
            P("space"),
            P("exc", "space"),
            P("exc", None, "space"),
        ),
        out_specs=(
            P("exc", None, "space"),
            P("exc", None, "space"),
            P(None, ("space", "exc")),
            P(None, ("space", "exc")),
        ),
        check_vma=False,
    )
```

```python
import functools

import jax
import jax.numpy as jnp
import ml_dtypes
import numpy as np
from jax import lax
from jax.experimental import pallas as pl
from jax.experimental.pallas import tpu as pltpu
from jax.sharding import PartitionSpec as P

STEPS = 4
LAYER = 128
TIME_STEP = 0.025
DAMPING = 0.5
GAIN = 6.0 * TIME_STEP
MESH = pl.DeviceIdType.MESH


def operator_table():
    points = np.array([-1.0, -1.0 / np.sqrt(5.0), 1.0 / np.sqrt(5.0), 1.0])
    barycentric = np.array(
        [1.0 / np.prod([points[j] - points[k] for k in range(4) if k != j]) for j in range(4)]
    )
    deriv = np.zeros((4, 4))
    for row in range(4):
        for column in range(4):
            if row != column:
                deriv[row, column] = (
                    barycentric[column] / barycentric[row] / (points[row] - points[column])
                )
        deriv[row, row] = -np.sum(deriv[row])
    identity = np.eye(4)
    along_x = 2.0 * np.kron(np.kron(deriv, identity), identity)
    along_y = 2.0 * np.kron(np.kron(identity, deriv), identity)
    along_z = 2.0 * np.kron(np.kron(identity, identity), deriv)
    curl = np.zeros((192, 192))
    curl[0:64, 64:128] = -along_z
    curl[0:64, 128:192] = along_y
    curl[64:128, 0:64] = along_z
    curl[64:128, 128:192] = -along_x
    curl[128:192, 0:64] = -along_y
    curl[128:192, 64:128] = along_x
    numbers = np.arange(64).reshape(4, 4, 4)
    faces = [
        numbers[0].ravel(),
        numbers[3].ravel(),
        numbers[:, 0].ravel(),
        numbers[:, 3].ravel(),
        numbers[:, :, 0].ravel(),
        numbers[:, :, 3].ravel(),
    ]
    inner = np.zeros((192, 192))
    for face in range(6):
        direction = face // 2
        sign = 1.0 if face % 2 else -1.0
        for component in range(3):
            for other in range(3):
                parity = (component - direction) * (direction - other) * (other - component) / 2.0
                for node in faces[face]:
                    inner[component * 64 + node, other * 64 + node] += sign * parity
    return inner - curl / 6.0


def split_table():
    table = operator_table()
    high = table.astype(ml_dtypes.bfloat16)
    low = (table - high.astype(np.float64)).astype(ml_dtypes.bfloat16)
    return np.concatenate([high, low], axis=0)


def split_faces():
    table = split_table()
    tables = []
    for start in (0, 48):
        rows = np.concatenate([np.arange(64, 80), np.arange(128, 144)]) + start
        high, low = table[0:192, rows], table[192:384, rows]
        tables.append(np.concatenate([high, low, high], axis=1))
    return np.stack(tables)


def halves(value):
    high = value.astype(jnp.bfloat16)
    low = (value - high.astype(jnp.float32)).astype(jnp.bfloat16)
    return high, low


def pick(value, index):
    index = jnp.broadcast_to(index, value.shape)
    return jnp.take_along_axis(value, index, axis=1, mode="promise_in_bounds")


def rows_of(ref, layer, start):
    return jnp.concatenate(
        [ref[layer, 64 + start : 80 + start], ref[layer, 128 + start : 144 + start]], axis=0
    )


def turn(trace, sign):
    return jnp.concatenate([sign * trace[16:32], -sign * trace[0:16]], axis=0)


def add_rows(ref, layer, start, value):
    ref[layer, 64 + start : 80 + start] += value[0:16]
    ref[layer, 128 + start : 144 + start] += value[16:32]


FAR_FIRST = (10, 6, 14, 2, 9, 11, 8, 5, 7, 13, 15, 1, 3, 4, 12)
MINE = (0, 48)
THEIRS = (48, 0)
SIGN = (-1.0, 1.0)


def kernel(
    n_exc,
    n_space,
    adj_e,
    adj_h,
    adj_j,
    fwd_e,
    inv_eps,
    drude,
    neighbor,
    design,
    ports,
    profile,
    table,
    face_table,
    out_e,
    out_h,
    out_eps,
    out_drude,
    e_ref,
    h_ref,
    j_ref,
    level_e,
    level_j,
    change_ref,
    late_ref,
    s_ref,
    z_ref,
    de_ref,
    f_ref,
    v_ref,
    w_ref,
    kick_ref,
    nb_ref,
    dm_ref,
    pe_ref,
    pp_ref,
    tb_ref,
    fb_ref,
    send_t,
    recv_t,
    recv_v,
    recv_nb,
    sums,
    parts,
    load_sem,
    send_sem,
    recv_sem,
    once_send_sem,
    once_recv_sem,
    part_send_sem,
    part_recv_sem,
    store_sem,
):
    me_exc = lax.axis_index("exc")
    me_space = lax.axis_index("space")
    left = lax.rem(me_space + n_space - 1, n_space)
    right = lax.rem(me_space + 1, n_space)
    own_rows = LAYER // n_exc
    f32 = jnp.float32

    barrier = pltpu.get_barrier_semaphore()
    for peer in (left, right):
        pl.semaphore_signal(barrier, inc=1, device_id={"space": peer}, device_id_type=MESH)

    loads = []

    def load(src, dst):
        copy = pltpu.make_async_copy(src, dst, load_sem.at[len(loads)])
        copy.start()
        loads.append(copy)
        return copy

    def load_layers(src, dst):
        return [load(src.at[..., pl.ds(n * LAYER, LAYER)], dst.at[n]) for n in range(2)]

    got_nb = load(neighbor, nb_ref)
    got_e = load_layers(adj_e.at[0], e_ref)
    got_tb = load(table, tb_ref)
    got_h = load_layers(adj_h.at[0], h_ref)
    got_v = load_layers(inv_eps, v_ref)
    got_w = load_layers(drude, w_ref)
    got_j = load_layers(adj_j.at[0], j_ref)
    got_pe = load(ports, pe_ref)
    got_pp = load(profile.at[0], pp_ref)
    got_fb = load(face_table, fb_ref)
    got_f = load_layers(fwd_e.at[0], f_ref)
    got_dm = load(design, dm_ref)

    for hop in range(1, n_exc):
        peer = lax.rem(me_exc + hop, n_exc)
        pl.semaphore_signal(barrier, inc=1, device_id={"exc": peer}, device_id_type=MESH)

    sublane = lax.broadcasted_iota(jnp.int32, (8, LAYER), 0)
    lower = sublane < 4
    first_k = (sublane & 3) == 0
    last_k = (sublane & 3) == 3

    z_ref[...] = jnp.zeros(z_ref.shape, f32)

    got_nb.wait()
    table_nb = nb_ref[...]
    place = table_nb & (LAYER - 1)

    def face(number, layer):
        return place[number : number + 1, layer * LAYER : (layer + 1) * LAYER]

    def inside(number, layer):
        cut = table_nb[number : number + 1, layer * LAYER : (layer + 1) * LAYER]
        return (cut >= 0).astype(f32)

    edge_y = [jnp.where(lower, face(3, n), face(2, n)) for n in range(2)]
    edge_z = [jnp.where(first_k, face(5, n), face(4, n)) for n in range(2)]
    along_y = [jnp.concatenate([index] * 8, axis=0) for index in edge_y]
    low_z = [face(4, n) for n in range(2)]
    high_z = [face(5, n) for n in range(2)]
    between = [face(1, 0), face(0, 1)]
    beyond = [face(0, 0), face(1, 1)]
    exists = [inside(0, 0), inside(1, 1)]

    def product(field):
        high, low = halves(field)
        whole = jnp.dot(tb_ref[...], high, preferred_element_type=f32)
        rest = jnp.dot(tb_ref[0:192, :], low, preferred_element_type=f32)
        return whole[0:192] + (whole[192:384] + rest)

    calls = []

    def local_flux(field_ref):
        total = product(jnp.concatenate([field_ref[0], field_ref[1]], axis=1))
        zeros = jnp.zeros((48, LAYER), f32)
        slot = len(calls) % 2
        calls.append(slot)
        result = []
        for n in range(2):
            far = pick(field_ref[n, pl.ds(0, 32, stride=4), :], high_z[n])
            z_ref[slot, n, pl.ds(3, 32, stride=4), :] = jnp.concatenate(
                [far[16:32], -far[0:16]], axis=0
            )
            near = pick(field_ref[n, pl.ds(3, 32, stride=4), :], low_z[n])
            z_ref[slot, n, pl.ds(0, 32, stride=4), :] = jnp.concatenate(
                [-near[16:32], near[0:16]], axis=0
            )
            own = field_ref[n].reshape(3, 4, 2, 8, LAYER)
            edge = jnp.concatenate(
                [
                    jnp.where(lower, own[0, :, 0], own[0, :, 1]),
                    jnp.where(lower, own[2, :, 0], own[2, :, 1]),
                ],
                axis=0,
            )
            outer = pick(edge.reshape(64, LAYER), along_y[n]).reshape(8, 8, LAYER)
            outer = pltpu.roll(outer, 4, 1)
            zero = jnp.zeros((4, 8, LAYER), f32)
            o_x, o_z = outer[0:4], outer[4:8]
            to_x = jnp.stack([jnp.where(lower, o_z, zero), jnp.where(lower, zero, -o_z)], axis=1)
            to_z = jnp.stack([jnp.where(lower, -o_x, zero), jnp.where(lower, zero, o_x)], axis=1)
            if n == 0:
                side = turn(pick(rows_of(field_ref, 1, 0), between[0]), 1.0)
                to_y = jnp.concatenate([zeros, side[0:16]], axis=0)
                to_z2 = jnp.concatenate([zeros, side[16:32]], axis=0)
            else:
                side = turn(pick(rows_of(field_ref, 0, 48), between[1]), -1.0)
                to_y = jnp.concatenate([side[0:16], zeros], axis=0)
                to_z2 = jnp.concatenate([side[16:32], zeros], axis=0)
            extra = jnp.concatenate(
                [
                    z_ref[slot, n, 0:64] + to_x.reshape(64, LAYER),
                    z_ref[slot, n, 64:128] + to_y,
                    to_z.reshape(64, LAYER) + to_z2,
                ],
                axis=0,
            )
            result.append(total[:, n * LAYER : (n + 1) * LAYER] + extra)
        return result

    def from_y(rows, index):
        outer = pltpu.roll(pick(jnp.where(lower, rows[0:8], rows[8:16]), index), 4, 0)
        zero = jnp.zeros((8, LAYER), f32)
        return jnp.concatenate(
            [jnp.where(lower, outer, zero), jnp.where(lower, zero, -outer)], axis=0
        )

    def from_z(rows, index):
        parts_z = []
        zero = jnp.zeros((8, LAYER), f32)
        for half in (rows[0:8], rows[8:16]):
            outer = pick(half, index)
            parts_z.append(
                jnp.where(last_k, pltpu.roll(outer, 3, 0), zero)
                - jnp.where(first_k, pltpu.roll(outer, 5, 0), zero)
            )
        return jnp.concatenate(parts_z, axis=0)

    def remote(src, dst, sems, side):
        copy = pltpu.make_async_remote_copy(
            src_ref=src,
            dst_ref=dst,
            send_sem=sems[0],
            recv_sem=sems[1],
            device_id={"space": (left, right)[side]},
            device_id_type=MESH,
        )
        copy.start()
        return copy

    sent = []

    def keep_trace(window, kind, ref):
        for side in range(2):
            send_t[window, kind, side] = rows_of(ref, side, MINE[side])

    def send_trace(window, kind):
        copies = []
        for side in range(2):
            copies.append(
                remote(
                    send_t.at[window, kind, side],
                    recv_t.at[window, kind, 1 - side],
                    (send_sem.at[window, kind, side], recv_sem.at[window, kind, 1 - side]),
                    side,
                )
            )
        sent.extend(copies)
        return copies

    sens = [[jnp.zeros((64, LAYER), f32)] * 2 for _ in range(2)]

    def add(kind, n, field, weight):
        term = (field * weight).reshape(3, 64, LAYER)
        sens[kind][n] = sens[kind][n] + (term[0] + term[1] + term[2])

    def change_of(n, step):
        return f_ref[n, step + 1].astype(f32) - f_ref[n, step].astype(f32)

    def add_eps(step):
        for n in range(2):
            add(0, n, level_e[step, n], change_of(n, step))

    def add_drude(step):
        for n in range(2):
            add(1, n, level_j[step, n], f_ref[n, step].astype(f32))

    def drive(step):
        for n in range(2):
            electric = (level_e[step - 1, n] if step else e_ref[n]).reshape(3, 64, LAYER)
            current = level_j[step - 1, n] if step else j_ref[n]
            current = (1.0 - TIME_STEP * DAMPING) * current.reshape(3, 64, LAYER)
            current = current + w_ref[n] * electric
            level_j[step, n] = current.reshape(192, LAYER)
            push = v_ref[n] * (current + s_ref[n].reshape(3, 64, LAYER))
            e_ref[n] = (electric - push).reshape(192, LAYER)

    def gather_pixels(stacked):
        pixel = lax.broadcasted_iota(jnp.int32, (LAYER, 2 * LAYER), 0)
        members = ((dm_ref[...] & (LAYER - 1)) == pixel).astype(jnp.bfloat16)
        high, low = halves(stacked)
        contract = (((1,), (1,)), ((), ()))
        return lax.dot_general(
            members, high, contract, preferred_element_type=f32
        ) + lax.dot_general(members, low, contract, preferred_element_type=f32)

    def kick(n, flux):
        return (kick_ref[n] * flux.reshape(3, 64, LAYER)).reshape(192, LAYER)

    ghost_y, ghost_z = [None, None], [None, None]

    for copy in got_e:
        copy.wait()

    for window in range(STEPS // 2):
        step = 2 * window
        field = e_ref if window == 0 else level_e.at[step - 1]
        keep_trace(window, 0, field)
        if window > 0:
            e0 = send_trace(window, 0)
        if window == 0:
            got_tb.wait()
        flux = local_flux(field)
        if window == 0:
            for copy in got_h:
                copy.wait()
        for n in range(2):
            h_ref[n] = h_ref[n] + GAIN * flux[n]
        keep_trace(window, 1, h_ref)
        if window == 0:
            pl.semaphore_wait(barrier, 2 + n_exc - 1)
            e0 = send_trace(window, 0)
        h1 = send_trace(window, 1)
        if window == 0:
            once = []
            for side in range(2):
                lanes = pl.ds(side * LAYER, LAYER)
                for at, (src, dst) in enumerate(((inv_eps, recv_v), (neighbor, recv_nb))):
                    once.append(
                        remote(
                            src.at[:, lanes],
                            dst.at[1 - side],
                            (once_send_sem.at[at, side], once_recv_sem.at[at, 1 - side]),
                            side,
                        )
                    )

        if window == 0:
            for copy in got_w + got_v + got_j + [got_pe, got_pp]:
                copy.wait()
            element = lax.broadcasted_iota(jnp.int32, (2 * LAYER, LAYER), 0)
            chosen = ((pe_ref[...] & (2 * LAYER - 1)) == element).astype(jnp.bfloat16)
            high, low = halves(pp_ref[...])
            contract = (((1,), (1,)), ((), ()))
            source = lax.dot_general(
                high, chosen, contract, preferred_element_type=f32
            ) + lax.dot_general(low, chosen, contract, preferred_element_type=f32)
            for n in range(2):
                s_ref[n] = source[:, n * LAYER : (n + 1) * LAYER]
                kick_ref[n] = GAIN * v_ref[n]
                v_ref[n] = TIME_STEP * v_ref[n]
                w_ref[n] = TIME_STEP * w_ref[n]
        drive(step)
        flux = local_flux(h_ref)
        for n in range(2):
            e_ref[n] = e_ref[n] - kick(n, flux[n])
        keep_trace(window, 2, e_ref)
        e1 = send_trace(window, 2)
        flux = local_flux(e_ref)
        for n in range(2):
            h_ref[n] = h_ref[n] + GAIN * flux[n]
        keep_trace(window, 3, h_ref)
        h2 = send_trace(window, 3)

        if window == 0:
            for copy in got_f + [got_fb, got_dm]:
                copy.wait()
        add_drude(step)
        if step + 2 < STEPS:
            pass
        else:
            add_eps(step - 2)
            add_eps(step - 1)
            add_drude(step - 1)
            for n in range(2):
                for at in range(2):
                    change_ref[at, n] = change_of(n, step + at)
                late_ref[n] = f_ref[n, step + 1].astype(f32)
        for copy in e0:
            copy.wait_recv()
        mine_dh, their_dh = [], []
        for side in range(2):
            sign = SIGN[side]
            outer = pick(recv_t[window, 0, side], beyond[side]) * exists[side]
            mine_dh.append(turn(outer, GAIN * sign))
            their_dh.append(turn(send_t[window, 0, side], -GAIN * sign))
        pairs = ((mine_dh[0], their_dh[1]), (mine_dh[1], their_dh[0]))
        spread = []
        for at in range(2):
            high, low = halves(jnp.concatenate(pairs[at], axis=1))
            spread.append(
                jnp.dot(
                    fb_ref[at],
                    jnp.concatenate([high, high, low], axis=0),
                    preferred_element_type=f32,
                )
            )

        def respond(side, ghost, across):
            layer = 2 + side if ghost else side
            start = THEIRS[side] if ghost else MINE[side]
            change = their_dh[side] if ghost else mine_dh[side]
            index_y = ghost_y[side] if ghost else edge_y[side]
            index_z = ghost_z[side] if ghost else edge_z[side]
            if ghost:
                out = spread[1 - side][:, LAYER : 2 * LAYER]
            else:
                out = spread[side][:, 0:LAYER]
            edge = from_y(change[16:32], index_y) + from_z(change[0:16], index_z)

            def with_face(rows, extra):
                end = start + 16
                middle = rows[start:end] + extra
                if start == 0:
                    return jnp.concatenate([middle, rows[end:64]], axis=0)
                return jnp.concatenate([rows[0:start], middle], axis=0)

            speed = kick_ref[layer]
            de_ref[layer, 0:64] = -speed * with_face(out[0:64], edge)
            de_ref[layer, 64:128] = -speed * with_face(out[64:128], across[0:16])
            de_ref[layer, 128:192] = -speed * with_face(out[128:192], across[16:32])

        def respond_ghosts():
            for side in range(2):
                across = send_t[window, 1, side] + mine_dh[side]
                respond(side, True, turn(across, -SIGN[side]))

        if window > 0:
            respond_ghosts()
        for copy in h1:
            copy.wait_recv()
        for side in range(2):
            across = (pick(recv_t[window, 1, side], beyond[side]) + their_dh[side]) * exists[side]
            respond(side, False, turn(across, SIGN[side]))
        for n in range(2):
            level_e[step, n] = e_ref[n] + de_ref[n]
            add_rows(h_ref, n, MINE[n], mine_dh[n])
        flux = local_flux(de_ref)
        for n in range(2):
            h_ref[n] = h_ref[n] + GAIN * flux[n]

        if window == 0:
            for copy in once:
                copy.wait_recv()
            for side in range(2):
                kick_ref[2 + side] = GAIN * pick(recv_v[side], beyond[side])
                far = recv_nb[side] & (LAYER - 1)
                back = jnp.broadcast_to(far[1 - side : 2 - side], (8, LAYER))

                def through(number):
                    rows = jnp.broadcast_to(far[number : number + 1], (8, LAYER))
                    return pick(back, pick(rows, beyond[side]))

                ghost_y[side] = jnp.where(lower, through(3), through(2))
                ghost_z[side] = jnp.where(first_k, through(5), through(4))
            respond_ghosts()

        def their_second():
            high, low = halves(jnp.concatenate([de_ref[2], de_ref[3]], axis=1))
            cuts = [tb_ref[at : at + 16, :] for at in (112, 176, 64, 128)]
            lows = [tb_ref[192 + at : 208 + at, :] for at in (112, 176, 64, 128)]
            whole = jnp.dot(jnp.concatenate(cuts + lows, axis=0), high, preferred_element_type=f32)
            rest = jnp.dot(jnp.concatenate(cuts, axis=0), low, preferred_element_type=f32)
            near = whole[0:64] + (whole[64:128] + rest)
            result = []
            for side in range(2):
                start = THEIRS[side]
                own = de_ref[2 + side, start : start + 16]
                edge = jnp.concatenate(
                    [-from_z(own, ghost_z[side]), -from_y(own, ghost_y[side])], axis=0
                )
                across = turn(rows_of(level_e.at[step], side, MINE[side]), -SIGN[side])
                lanes = slice(side * LAYER, (side + 1) * LAYER)
                at = slice(32 * side, 32 * side + 32)
                result.append(their_dh[side] + GAIN * (near[at, lanes] + edge + across))
            return result

        for copy in e1:
            copy.wait_recv()
        for side in range(2):
            outer = pick(recv_t[window, 2, side], beyond[side])
            outer = (outer + rows_of(de_ref, 2 + side, THEIRS[side])) * exists[side]
            add_rows(h_ref, side, MINE[side], turn(outer, GAIN * SIGN[side]))
        if step + 2 == STEPS:
            stores = []
            for n in range(2):
                lanes = pl.ds(n * LAYER, LAYER)
                copy = pltpu.make_async_copy(h_ref.at[n], out_h.at[0, :, lanes], store_sem.at[n])
                copy.start()
                stores.append(copy)

        drive(step + 1)
        flux = local_flux(h_ref)
        for n in range(2):
            level_e[step + 1, n] = e_ref[n] - kick(n, flux[n])
        if step + 2 == STEPS:
            for n in range(2):
                add(0, n, level_e[step, n], change_ref[0, n])
                add(1, n, level_j[step + 1, n], late_ref[n])
            sums[...] = gather_pixels(
                jnp.concatenate(
                    [jnp.concatenate(sens[0], axis=1), jnp.concatenate(sens[1], axis=1)], axis=0
                )
            )
        their_dh2 = their_second()
        for copy in h2:
            copy.wait_recv()
        for side in range(2):
            outer = pick(recv_t[window, 3, side], beyond[side])
            outer = turn((outer + their_dh2[side]) * exists[side], -SIGN[side])
            speed = kick_ref[side, MINE[side] : MINE[side] + 16]
            add_rows(
                level_e.at[step + 1],
                side,
                MINE[side],
                jnp.concatenate([speed * outer[0:16], speed * outer[16:32]], axis=0),
            )

    for n in range(2):
        lanes = pl.ds(n * LAYER, LAYER)
        copy = pltpu.make_async_copy(
            level_e.at[STEPS - 1, n], out_e.at[0, :, lanes], store_sem.at[2 + n]
        )
        copy.start()
        stores.append(copy)
    sens[0] = [jnp.zeros((64, LAYER), f32)] * 2
    for n in range(2):
        add(0, n, level_e[STEPS - 1, n], change_ref[1, n])
    sums[:, 0:64] += gather_pixels(jnp.concatenate(sens[0], axis=1))
    part_copies = {}
    for hop in FAR_FIRST if n_exc == 16 else range(1, n_exc):
        peer = lax.rem(me_exc + hop, n_exc)
        start = pl.multiple_of(peer * own_rows, own_rows)
        copy = pltpu.make_async_remote_copy(
            src_ref=sums.at[pl.ds(start, own_rows)],
            dst_ref=parts.at[hop],
            send_sem=part_send_sem.at[hop],
            recv_sem=part_recv_sem.at[hop],
            device_id={"exc": peer},
            device_id_type=MESH,
        )
        copy.start()
        part_copies[hop] = copy
    for copy in sent + once:
        copy.wait_send()
    total = sums[pl.ds(pl.multiple_of(me_exc * own_rows, own_rows), own_rows)]
    for hop in range(1, n_exc):
        part_copies[hop].wait_recv()
        total = total + parts[hop]
    total = total * (1.0 / n_exc)
    out_eps[...] = total[:, 0:64]
    out_drude[...] = total[:, 64:128]
    for copy in part_copies.values():
        copy.wait_send()
    for copy in stores:
        copy.wait()


def write_kernel(e_in, h_in, a_in, b_in, e_out, h_out, a_out, b_out, sem):
    copies = [
        pltpu.make_async_copy(src, dst, sem.at[at])
        for at, (src, dst) in enumerate(
            ((e_in, e_out), (h_in, h_out), (a_in, a_out), (b_in, b_out))
        )
    ]
    for copy in copies:
        copy.start()
    for copy in copies:
        copy.wait()


def write(*arrays):
    spec = pl.BlockSpec(memory_space=pltpu.HBM)
    return pl.pallas_call(
        write_kernel,
        out_shape=tuple(jax.ShapeDtypeStruct(a.shape, a.dtype) for a in arrays),
        in_specs=[pl.BlockSpec(memory_space=pltpu.VMEM)] * 4,
        out_specs=(spec,) * 4,
        scratch_shapes=[pltpu.SemaphoreType.DMA((4,))],
        compiler_params=pltpu.CompilerParams(vmem_limit_bytes=2 << 20),
        name="write_out",
    )(*arrays)


def local(n_exc, n_space, *args):
    (adj_e, adj_h, adj_j, fwd_e, inv_eps, drude, neighbor, design, ports, profile) = args
    own_rows = LAYER // n_exc
    f32 = jnp.float32
    anywhere = pl.BlockSpec(memory_space=pltpu.HBM)
    in_vmem = pl.BlockSpec(memory_space=pltpu.VMEM)
    new_e, new_h, grad_eps, grad_drude = pl.pallas_call(
        functools.partial(kernel, n_exc, n_space),
        out_shape=(
            jax.ShapeDtypeStruct(adj_e.shape, f32),
            jax.ShapeDtypeStruct(adj_h.shape, f32),
            jax.ShapeDtypeStruct((own_rows, 64), f32),
            jax.ShapeDtypeStruct((own_rows, 64), f32),
        ),
        in_specs=[anywhere] * 12,
        out_specs=(anywhere, anywhere, in_vmem, in_vmem),
        scratch_shapes=[
            pltpu.VMEM((2, 192, LAYER), f32),
            pltpu.VMEM((2, 192, LAYER), f32),
            pltpu.VMEM((2, 192, LAYER), f32),
            pltpu.VMEM((STEPS, 2, 192, LAYER), f32),
            pltpu.VMEM((STEPS, 2, 192, LAYER), f32),
            pltpu.VMEM((2, 2, 192, LAYER), f32),
            pltpu.VMEM((2, 192, LAYER), f32),
            pltpu.VMEM((2, 192, LAYER), f32),
            pltpu.VMEM((2, 2, LAYER, LAYER), f32),
            pltpu.VMEM((4, 192, LAYER), f32),
            pltpu.VMEM((2, STEPS + 1, 192, LAYER), jnp.bfloat16),
            pltpu.VMEM((2, 64, LAYER), f32),
            pltpu.VMEM((2, 64, LAYER), f32),
            pltpu.VMEM((4, 64, LAYER), f32),
            pltpu.VMEM((6, 2 * LAYER), jnp.int32),
            pltpu.VMEM((1, 2 * LAYER), jnp.int32),
            pltpu.VMEM((1, LAYER), jnp.int32),
            pltpu.VMEM((192, LAYER), f32),
            pltpu.VMEM((384, 192), jnp.bfloat16),
            pltpu.VMEM((2, 192, 96), jnp.bfloat16),
            pltpu.VMEM((STEPS // 2, 4, 2, 32, LAYER), f32),
            pltpu.VMEM((STEPS // 2, 4, 2, 32, LAYER), f32),
            pltpu.VMEM((2, 64, LAYER), f32),
            pltpu.VMEM((2, 6, LAYER), jnp.int32),
            pltpu.VMEM((LAYER, LAYER), f32),
            pltpu.VMEM((n_exc, own_rows, LAYER), f32),
            pltpu.SemaphoreType.DMA((24,)),
            pltpu.SemaphoreType.DMA((STEPS // 2, 4, 2)),
            pltpu.SemaphoreType.DMA((STEPS // 2, 4, 2)),
            pltpu.SemaphoreType.DMA((2, 2)),
            pltpu.SemaphoreType.DMA((2, 2)),
            pltpu.SemaphoreType.DMA((n_exc,)),
            pltpu.SemaphoreType.DMA((n_exc,)),
            pltpu.SemaphoreType.DMA((4,)),
        ],
        compiler_params=pltpu.CompilerParams(
            collective_id=0, has_side_effects=True, vmem_limit_bytes=16 << 20
        ),
        name="adjoint_steps",
    )(
        *[pltpu.with_memory_space_constraint(x, pltpu.HBM) for x in (adj_e, adj_h, adj_j, fwd_e, inv_eps, drude, neighbor, design.reshape(1, 2 * LAYER), ports, profile, jnp.asarray(split_table()), jnp.asarray(split_faces()))]
    )
    new_e, new_h, grad_eps, grad_drude = write(new_e, new_h, grad_eps, grad_drude)
    return new_e, new_h, grad_eps.T, grad_drude.T


def solution(mesh):
    return jax.shard_map(
        functools.partial(local, mesh.shape["exc"], mesh.shape["space"]),
        mesh=mesh,
        in_specs=(
            P("exc", None, "space"),
            P("exc", None, "space"),
            P("exc", None, "space"),
            P("exc", None, None, "space"),
            P(None, "space"),
            P(None, "space"),
            P(None, "space"),
            P("space"),
            P("exc", "space"),
            P("exc", None, "space"),
        ),
        out_specs=(
            P("exc", None, "space"),
            P("exc", None, "space"),
            P(None, ("space", "exc")),
            P(None, ("space", "exc")),
        ),
        check_vma=False,
    )
```

```python
import functools

import jax
import jax.numpy as jnp
import ml_dtypes
import numpy as np
from jax import lax
from jax.experimental import pallas as pl
from jax.experimental.pallas import tpu as pltpu
from jax.sharding import PartitionSpec as P

STEPS = 4
LAYER = 128
TIME_STEP = 0.025
DAMPING = 0.5
GAIN = 6.0 * TIME_STEP
MESH = pl.DeviceIdType.MESH


def operator_table():
    points = np.array([-1.0, -1.0 / np.sqrt(5.0), 1.0 / np.sqrt(5.0), 1.0])
    barycentric = np.array(
        [1.0 / np.prod([points[j] - points[k] for k in range(4) if k != j]) for j in range(4)]
    )
    deriv = np.zeros((4, 4))
    for row in range(4):
        for column in range(4):
            if row != column:
                deriv[row, column] = (
                    barycentric[column] / barycentric[row] / (points[row] - points[column])
                )
        deriv[row, row] = -np.sum(deriv[row])
    identity = np.eye(4)
    along_x = 2.0 * np.kron(np.kron(deriv, identity), identity)
    along_y = 2.0 * np.kron(np.kron(identity, deriv), identity)
    along_z = 2.0 * np.kron(np.kron(identity, identity), deriv)
    curl = np.zeros((192, 192))
    curl[0:64, 64:128] = -along_z
    curl[0:64, 128:192] = along_y
    curl[64:128, 0:64] = along_z
    curl[64:128, 128:192] = -along_x
    curl[128:192, 0:64] = -along_y
    curl[128:192, 64:128] = along_x
    numbers = np.arange(64).reshape(4, 4, 4)
    faces = [
        numbers[0].ravel(),
        numbers[3].ravel(),
        numbers[:, 0].ravel(),
        numbers[:, 3].ravel(),
        numbers[:, :, 0].ravel(),
        numbers[:, :, 3].ravel(),
    ]
    inner = np.zeros((192, 192))
    for face in range(6):
        direction = face // 2
        sign = 1.0 if face % 2 else -1.0
        for component in range(3):
            for other in range(3):
                parity = (component - direction) * (direction - other) * (other - component) / 2.0
                for node in faces[face]:
                    inner[component * 64 + node, other * 64 + node] += sign * parity
    return inner - curl / 6.0


def split_table():
    table = operator_table()
    high = table.astype(ml_dtypes.bfloat16)
    low = (table - high.astype(np.float64)).astype(ml_dtypes.bfloat16)
    return np.concatenate([high, low], axis=0)


def split_faces():
    table = split_table()
    tables = []
    for start in (0, 48):
        rows = np.concatenate([np.arange(64, 80), np.arange(128, 144)]) + start
        high, low = table[0:192, rows], table[192:384, rows]
        tables.append(np.concatenate([high, low, high], axis=1))
    return np.stack(tables)


def halves(value):
    high = value.astype(jnp.bfloat16)
    low = (value - high.astype(jnp.float32)).astype(jnp.bfloat16)
    return high, low


def pick(value, index):
    index = jnp.broadcast_to(index, value.shape)
    return jnp.take_along_axis(value, index, axis=1, mode="promise_in_bounds")


def rows_of(ref, layer, start):
    return jnp.concatenate(
        [ref[layer, 64 + start : 80 + start], ref[layer, 128 + start : 144 + start]], axis=0
    )


def turn(trace, sign):
    return jnp.concatenate([sign * trace[16:32], -sign * trace[0:16]], axis=0)


def add_rows(ref, layer, start, value):
    ref[layer, 64 + start : 80 + start] += value[0:16]
    ref[layer, 128 + start : 144 + start] += value[16:32]


FAR_FIRST = (10, 6, 14, 2, 9, 11, 8, 5, 7, 13, 15, 1, 3, 4, 12)
MINE = (0, 48)
THEIRS = (48, 0)
SIGN = (-1.0, 1.0)


def kernel(
    n_exc,
    n_space,
    adj_e,
    adj_h,
    adj_j,
    fwd_e,
    inv_eps,
    drude,
    neighbor,
    design,
    ports,
    profile,
    table,
    face_table,
    out_e,
    out_h,
    out_eps,
    out_drude,
    e_ref,
    h_ref,
    j_ref,
    level_e,
    level_j,
    change_ref,
    late_ref,
    s_ref,
    z_ref,
    de_ref,
    f_ref,
    v_ref,
    w_ref,
    kick_ref,
    nb_ref,
    dm_ref,
    pe_ref,
    pp_ref,
    tb_ref,
    fb_ref,
    send_t,
    recv_t,
    recv_v,
    recv_nb,
    sums,
    parts,
    load_sem,
    send_sem,
    recv_sem,
    once_send_sem,
    once_recv_sem,
    part_send_sem,
    part_recv_sem,
    store_sem,
):
    me_exc = lax.axis_index("exc")
    me_space = lax.axis_index("space")
    left = lax.rem(me_space + n_space - 1, n_space)
    right = lax.rem(me_space + 1, n_space)
    own_rows = LAYER // n_exc
    f32 = jnp.float32

    barrier = pltpu.get_barrier_semaphore()
    has = (me_space > 0, me_space < n_space - 1)
    for side, peer in enumerate((left, right)):

        @pl.when(has[side])
        def _():
            pl.semaphore_signal(barrier, inc=1, device_id={"space": peer}, device_id_type=MESH)


    loads = []

    def load(src, dst):
        copy = pltpu.make_async_copy(src, dst, load_sem.at[len(loads)])
        copy.start()
        loads.append(copy)
        return copy

    def load_layers(src, dst):
        return [load(src.at[..., pl.ds(n * LAYER, LAYER)], dst.at[n]) for n in range(2)]

    got_nb = load(neighbor, nb_ref)
    got_e = load_layers(adj_e.at[0], e_ref)
    got_tb = load(table, tb_ref)
    got_h = load_layers(adj_h.at[0], h_ref)
    got_v = load_layers(inv_eps, v_ref)
    got_w = load_layers(drude, w_ref)
    got_j = load_layers(adj_j.at[0], j_ref)
    got_pe = load(ports, pe_ref)
    got_pp = load(profile.at[0], pp_ref)
    got_fb = load(face_table, fb_ref)
    got_f = load_layers(fwd_e.at[0], f_ref)
    got_dm = load(design, dm_ref)

    for hop in range(1, n_exc):
        peer = lax.rem(me_exc + hop, n_exc)
        pl.semaphore_signal(barrier, inc=1, device_id={"exc": peer}, device_id_type=MESH)

    sublane = lax.broadcasted_iota(jnp.int32, (8, LAYER), 0)
    lower = sublane < 4
    first_k = (sublane & 3) == 0
    last_k = (sublane & 3) == 3

    z_ref[...] = jnp.zeros(z_ref.shape, f32)
    for side in range(2):

        @pl.when(jnp.logical_not(has[side]))
        def _():
            for window in range(STEPS // 2):
                for kind in range(4):
                    recv_t[window, kind, side] = jnp.zeros((32, LAYER), f32)
            recv_v[side] = jnp.zeros((64, LAYER), f32)
            recv_nb[side] = jnp.zeros((6, LAYER), jnp.int32)


    got_nb.wait()
    table_nb = nb_ref[...]
    place = table_nb & (LAYER - 1)

    def face(number, layer):
        return place[number : number + 1, layer * LAYER : (layer + 1) * LAYER]

    def inside(number, layer):
        cut = table_nb[number : number + 1, layer * LAYER : (layer + 1) * LAYER]
        return (cut >= 0).astype(f32)

    edge_y = [jnp.where(lower, face(3, n), face(2, n)) for n in range(2)]
    edge_z = [jnp.where(first_k, face(5, n), face(4, n)) for n in range(2)]
    along_y = [jnp.concatenate([index] * 8, axis=0) for index in edge_y]
    low_z = [face(4, n) for n in range(2)]
    high_z = [face(5, n) for n in range(2)]
    between = [face(1, 0), face(0, 1)]
    beyond = [face(0, 0), face(1, 1)]
    exists = [inside(0, 0), inside(1, 1)]

    def product(field):
        high, low = halves(field)
        whole = jnp.dot(tb_ref[...], high, preferred_element_type=f32)
        rest = jnp.dot(tb_ref[0:192, :], low, preferred_element_type=f32)
        return whole[0:192] + (whole[192:384] + rest)

    calls = []

    def local_flux(field_ref):
        total = product(jnp.concatenate([field_ref[0], field_ref[1]], axis=1))
        zeros = jnp.zeros((48, LAYER), f32)
        slot = len(calls) % 2
        calls.append(slot)
        result = []
        for n in range(2):
            far = pick(field_ref[n, pl.ds(0, 32, stride=4), :], high_z[n])
            z_ref[slot, n, pl.ds(3, 32, stride=4), :] = jnp.concatenate(
                [far[16:32], -far[0:16]], axis=0
            )
            near = pick(field_ref[n, pl.ds(3, 32, stride=4), :], low_z[n])
            z_ref[slot, n, pl.ds(0, 32, stride=4), :] = jnp.concatenate(
                [-near[16:32], near[0:16]], axis=0
            )
            own = field_ref[n].reshape(3, 4, 2, 8, LAYER)
            edge = jnp.concatenate(
                [
                    jnp.where(lower, own[0, :, 0], own[0, :, 1]),
                    jnp.where(lower, own[2, :, 0], own[2, :, 1]),
                ],
                axis=0,
            )
            outer = pick(edge.reshape(64, LAYER), along_y[n]).reshape(8, 8, LAYER)
            outer = pltpu.roll(outer, 4, 1)
            zero = jnp.zeros((4, 8, LAYER), f32)
            o_x, o_z = outer[0:4], outer[4:8]
            to_x = jnp.stack([jnp.where(lower, o_z, zero), jnp.where(lower, zero, -o_z)], axis=1)
            to_z = jnp.stack([jnp.where(lower, -o_x, zero), jnp.where(lower, zero, o_x)], axis=1)
            if n == 0:
                side = turn(pick(rows_of(field_ref, 1, 0), between[0]), 1.0)
                to_y = jnp.concatenate([zeros, side[0:16]], axis=0)
                to_z2 = jnp.concatenate([zeros, side[16:32]], axis=0)
            else:
                side = turn(pick(rows_of(field_ref, 0, 48), between[1]), -1.0)
                to_y = jnp.concatenate([side[0:16], zeros], axis=0)
                to_z2 = jnp.concatenate([side[16:32], zeros], axis=0)
            extra = jnp.concatenate(
                [
                    z_ref[slot, n, 0:64] + to_x.reshape(64, LAYER),
                    z_ref[slot, n, 64:128] + to_y,
                    to_z.reshape(64, LAYER) + to_z2,
                ],
                axis=0,
            )
            result.append(total[:, n * LAYER : (n + 1) * LAYER] + extra)
        return result

    def from_y(rows, index):
        outer = pltpu.roll(pick(jnp.where(lower, rows[0:8], rows[8:16]), index), 4, 0)
        zero = jnp.zeros((8, LAYER), f32)
        return jnp.concatenate(
            [jnp.where(lower, outer, zero), jnp.where(lower, zero, -outer)], axis=0
        )

    def from_z(rows, index):
        parts_z = []
        zero = jnp.zeros((8, LAYER), f32)
        for half in (rows[0:8], rows[8:16]):
            outer = pick(half, index)
            parts_z.append(
                jnp.where(last_k, pltpu.roll(outer, 3, 0), zero)
                - jnp.where(first_k, pltpu.roll(outer, 5, 0), zero)
            )
        return jnp.concatenate(parts_z, axis=0)

    def remote(src, dst, sems, side):
        copy = pltpu.make_async_remote_copy(
            src_ref=src,
            dst_ref=dst,
            send_sem=sems[0],
            recv_sem=sems[1],
            device_id={"space": (left, right)[side]},
            device_id_type=MESH,
        )

        @pl.when(has[side])
        def _():
            copy.start()

        return copy, side

    def arrive(copies):
        for copy, side in copies:
            pl.when(has[1 - side])(copy.wait_recv)

    def leave(copies):
        for copy, side in copies:
            pl.when(has[side])(copy.wait_send)

    sent = []

    def keep_trace(window, kind, ref):
        for side in range(2):
            send_t[window, kind, side] = rows_of(ref, side, MINE[side])

    def send_trace(window, kind):
        copies = []
        for side in range(2):
            copies.append(
                remote(
                    send_t.at[window, kind, side],
                    recv_t.at[window, kind, 1 - side],
                    (send_sem.at[window, kind, side], recv_sem.at[window, kind, 1 - side]),
                    side,
                )
            )
        sent.extend(copies)
        return copies

    sens = [[jnp.zeros((64, LAYER), f32)] * 2 for _ in range(2)]

    def add(kind, n, field, weight):
        term = (field * weight).reshape(3, 64, LAYER)
        sens[kind][n] = sens[kind][n] + (term[0] + term[1] + term[2])

    def change_of(n, step):
        return f_ref[n, step + 1].astype(f32) - f_ref[n, step].astype(f32)

    def add_eps(step):
        for n in range(2):
            add(0, n, level_e[step, n], change_of(n, step))

    def add_drude(step):
        for n in range(2):
            add(1, n, level_j[step, n], f_ref[n, step].astype(f32))

    def drive(step):
        for n in range(2):
            electric = (level_e[step - 1, n] if step else e_ref[n]).reshape(3, 64, LAYER)
            current = level_j[step - 1, n] if step else j_ref[n]
            current = (1.0 - TIME_STEP * DAMPING) * current.reshape(3, 64, LAYER)
            current = current + w_ref[n] * electric
            level_j[step, n] = current.reshape(192, LAYER)
            push = v_ref[n] * (current + s_ref[n].reshape(3, 64, LAYER))
            e_ref[n] = (electric - push).reshape(192, LAYER)

    def gather_pixels(stacked):
        pixel = lax.broadcasted_iota(jnp.int32, (LAYER, 2 * LAYER), 0)
        members = ((dm_ref[...] & (LAYER - 1)) == pixel).astype(jnp.bfloat16)
        high, low = halves(stacked)
        contract = (((1,), (1,)), ((), ()))
        return lax.dot_general(
            members, high, contract, preferred_element_type=f32
        ) + lax.dot_general(members, low, contract, preferred_element_type=f32)

    def kick(n, flux):
        return (kick_ref[n] * flux.reshape(3, 64, LAYER)).reshape(192, LAYER)

    ghost_y, ghost_z = [None, None], [None, None]

    for copy in got_e:
        copy.wait()

    for window in range(STEPS // 2):
        step = 2 * window
        field = e_ref if window == 0 else level_e.at[step - 1]
        keep_trace(window, 0, field)
        if window > 0:
            e0 = send_trace(window, 0)
        if window == 0:
            got_tb.wait()
        flux = local_flux(field)
        if window == 0:
            for copy in got_h:
                copy.wait()
        for n in range(2):
            h_ref[n] = h_ref[n] + GAIN * flux[n]
        keep_trace(window, 1, h_ref)
        if window == 0:
            arrivals = has[0].astype(jnp.int32) + has[1].astype(jnp.int32)
            pl.semaphore_wait(barrier, arrivals + (n_exc - 1))
            e0 = send_trace(window, 0)
        h1 = send_trace(window, 1)
        if window == 0:
            once = []
            for side in range(2):
                lanes = pl.ds(side * LAYER, LAYER)
                for at, (src, dst) in enumerate(((inv_eps, recv_v), (neighbor, recv_nb))):
                    once.append(
                        remote(
                            src.at[:, lanes],
                            dst.at[1 - side],
                            (once_send_sem.at[at, side], once_recv_sem.at[at, 1 - side]),
                            side,
                        )
                    )

        if window == 0:
            for copy in got_w + got_v + got_j + [got_pe, got_pp]:
                copy.wait()
            element = lax.broadcasted_iota(jnp.int32, (2 * LAYER, LAYER), 0)
            chosen = ((pe_ref[...] & (2 * LAYER - 1)) == element).astype(jnp.bfloat16)
            high, low = halves(pp_ref[...])
            contract = (((1,), (1,)), ((), ()))
            source = lax.dot_general(
                high, chosen, contract, preferred_element_type=f32
            ) + lax.dot_general(low, chosen, contract, preferred_element_type=f32)
            for n in range(2):
                s_ref[n] = source[:, n * LAYER : (n + 1) * LAYER]
                kick_ref[n] = GAIN * v_ref[n]
                v_ref[n] = TIME_STEP * v_ref[n]
                w_ref[n] = TIME_STEP * w_ref[n]
        drive(step)
        flux = local_flux(h_ref)
        for n in range(2):
            e_ref[n] = e_ref[n] - kick(n, flux[n])
        keep_trace(window, 2, e_ref)
        e1 = send_trace(window, 2)
        flux = local_flux(e_ref)
        for n in range(2):
            h_ref[n] = h_ref[n] + GAIN * flux[n]
        keep_trace(window, 3, h_ref)
        h2 = send_trace(window, 3)

        if window == 0:
            for copy in got_f + [got_fb, got_dm]:
                copy.wait()
        add_drude(step)
        if step + 2 < STEPS:
            pass
        else:
            add_eps(step - 2)
            add_eps(step - 1)
            add_drude(step - 1)
            for n in range(2):
                for at in range(2):
                    change_ref[at, n] = change_of(n, step + at)
                late_ref[n] = f_ref[n, step + 1].astype(f32)
        arrive(e0)
        mine_dh, their_dh = [], []
        for side in range(2):
            sign = SIGN[side]
            outer = pick(recv_t[window, 0, side], beyond[side]) * exists[side]
            mine_dh.append(turn(outer, GAIN * sign))
            their_dh.append(turn(send_t[window, 0, side], -GAIN * sign))
        pairs = ((mine_dh[0], their_dh[1]), (mine_dh[1], their_dh[0]))
        spread = []
        for at in range(2):
            high, low = halves(jnp.concatenate(pairs[at], axis=1))
            spread.append(
                jnp.dot(
                    fb_ref[at],
                    jnp.concatenate([high, high, low], axis=0),
                    preferred_element_type=f32,
                )
            )

        def respond(side, ghost, across):
            layer = 2 + side if ghost else side
            start = THEIRS[side] if ghost else MINE[side]
            change = their_dh[side] if ghost else mine_dh[side]
            index_y = ghost_y[side] if ghost else edge_y[side]
            index_z = ghost_z[side] if ghost else edge_z[side]
            if ghost:
                out = spread[1 - side][:, LAYER : 2 * LAYER]
            else:
                out = spread[side][:, 0:LAYER]
            edge = from_y(change[16:32], index_y) + from_z(change[0:16], index_z)

            def with_face(rows, extra):
                end = start + 16
                middle = rows[start:end] + extra
                if start == 0:
                    return jnp.concatenate([middle, rows[end:64]], axis=0)
                return jnp.concatenate([rows[0:start], middle], axis=0)

            speed = kick_ref[layer]
            de_ref[layer, 0:64] = -speed * with_face(out[0:64], edge)
            de_ref[layer, 64:128] = -speed * with_face(out[64:128], across[0:16])
            de_ref[layer, 128:192] = -speed * with_face(out[128:192], across[16:32])

        def respond_ghosts():
            for side in range(2):
                across = send_t[window, 1, side] + mine_dh[side]
                respond(side, True, turn(across, -SIGN[side]))

        if window > 0:
            respond_ghosts()
        arrive(h1)
        for side in range(2):
            across = (pick(recv_t[window, 1, side], beyond[side]) + their_dh[side]) * exists[side]
            respond(side, False, turn(across, SIGN[side]))
        for n in range(2):
            level_e[step, n] = e_ref[n] + de_ref[n]
            add_rows(h_ref, n, MINE[n], mine_dh[n])
        flux = local_flux(de_ref)
        for n in range(2):
            h_ref[n] = h_ref[n] + GAIN * flux[n]

        if window == 0:
            arrive(once)
            for side in range(2):
                kick_ref[2 + side] = GAIN * pick(recv_v[side], beyond[side])
                far = recv_nb[side] & (LAYER - 1)
                back = jnp.broadcast_to(far[1 - side : 2 - side], (8, LAYER))

                def through(number):
                    rows = jnp.broadcast_to(far[number : number + 1], (8, LAYER))
                    return pick(back, pick(rows, beyond[side]))

                ghost_y[side] = jnp.where(lower, through(3), through(2))
                ghost_z[side] = jnp.where(first_k, through(5), through(4))
            respond_ghosts()

        def their_second():
            high, low = halves(jnp.concatenate([de_ref[2], de_ref[3]], axis=1))
            cuts = [tb_ref[at : at + 16, :] for at in (112, 176, 64, 128)]
            lows = [tb_ref[192 + at : 208 + at, :] for at in (112, 176, 64, 128)]
            whole = jnp.dot(jnp.concatenate(cuts + lows, axis=0), high, preferred_element_type=f32)
            rest = jnp.dot(jnp.concatenate(cuts, axis=0), low, preferred_element_type=f32)
            near = whole[0:64] + (whole[64:128] + rest)
            result = []
            for side in range(2):
                start = THEIRS[side]
                own = de_ref[2 + side, start : start + 16]
                edge = jnp.concatenate(
                    [-from_z(own, ghost_z[side]), -from_y(own, ghost_y[side])], axis=0
                )
                across = turn(rows_of(level_e.at[step], side, MINE[side]), -SIGN[side])
                lanes = slice(side * LAYER, (side + 1) * LAYER)
                at = slice(32 * side, 32 * side + 32)
                result.append(their_dh[side] + GAIN * (near[at, lanes] + edge + across))
            return result

        arrive(e1)
        for side in range(2):
            outer = pick(recv_t[window, 2, side], beyond[side])
            outer = (outer + rows_of(de_ref, 2 + side, THEIRS[side])) * exists[side]
            add_rows(h_ref, side, MINE[side], turn(outer, GAIN * SIGN[side]))
        if step + 2 == STEPS:
            stores = []
            for n in range(2):
                lanes = pl.ds(n * LAYER, LAYER)
                copy = pltpu.make_async_copy(h_ref.at[n], out_h.at[0, :, lanes], store_sem.at[n])
                copy.start()
                stores.append(copy)

        drive(step + 1)
        flux = local_flux(h_ref)
        for n in range(2):
            level_e[step + 1, n] = e_ref[n] - kick(n, flux[n])
        if step + 2 == STEPS:
            for n in range(2):
                add(0, n, level_e[step, n], change_ref[0, n])
                add(1, n, level_j[step + 1, n], late_ref[n])
            sums[...] = gather_pixels(
                jnp.concatenate(
                    [jnp.concatenate(sens[0], axis=1), jnp.concatenate(sens[1], axis=1)], axis=0
                )
            )
        their_dh2 = their_second()
        arrive(h2)
        for side in range(2):
            outer = pick(recv_t[window, 3, side], beyond[side])
            outer = turn((outer + their_dh2[side]) * exists[side], -SIGN[side])
            speed = kick_ref[side, MINE[side] : MINE[side] + 16]
            add_rows(
                level_e.at[step + 1],
                side,
                MINE[side],
                jnp.concatenate([speed * outer[0:16], speed * outer[16:32]], axis=0),
            )

    for n in range(2):
        lanes = pl.ds(n * LAYER, LAYER)
        copy = pltpu.make_async_copy(
            level_e.at[STEPS - 1, n], out_e.at[0, :, lanes], store_sem.at[2 + n]
        )
        copy.start()
        stores.append(copy)
    sens[0] = [jnp.zeros((64, LAYER), f32)] * 2
    for n in range(2):
        add(0, n, level_e[STEPS - 1, n], change_ref[1, n])
    sums[:, 0:64] += gather_pixels(jnp.concatenate(sens[0], axis=1))
    part_copies = {}
    for hop in FAR_FIRST if n_exc == 16 else range(1, n_exc):
        peer = lax.rem(me_exc + hop, n_exc)
        start = pl.multiple_of(peer * own_rows, own_rows)
        copy = pltpu.make_async_remote_copy(
            src_ref=sums.at[pl.ds(start, own_rows)],
            dst_ref=parts.at[hop],
            send_sem=part_send_sem.at[hop],
            recv_sem=part_recv_sem.at[hop],
            device_id={"exc": peer},
            device_id_type=MESH,
        )
        copy.start()
        part_copies[hop] = copy
    leave(sent + once)
    total = sums[pl.ds(pl.multiple_of(me_exc * own_rows, own_rows), own_rows)]
    for hop in range(1, n_exc):
        part_copies[hop].wait_recv()
        total = total + parts[hop]
    total = total * (1.0 / n_exc)
    out_eps[...] = total[:, 0:64]
    out_drude[...] = total[:, 64:128]
    for copy in part_copies.values():
        copy.wait_send()
    for copy in stores:
        copy.wait()


def write_kernel(e_in, h_in, a_in, b_in, e_out, h_out, a_out, b_out, sem):
    copies = [
        pltpu.make_async_copy(src, dst, sem.at[at])
        for at, (src, dst) in enumerate(
            ((e_in, e_out), (h_in, h_out), (a_in, a_out), (b_in, b_out))
        )
    ]
    for copy in copies:
        copy.start()
    for copy in copies:
        copy.wait()


def write(*arrays):
    spec = pl.BlockSpec(memory_space=pltpu.HBM)
    return pl.pallas_call(
        write_kernel,
        out_shape=tuple(jax.ShapeDtypeStruct(a.shape, a.dtype) for a in arrays),
        in_specs=[pl.BlockSpec(memory_space=pltpu.VMEM)] * 4,
        out_specs=(spec,) * 4,
        scratch_shapes=[pltpu.SemaphoreType.DMA((4,))],
        compiler_params=pltpu.CompilerParams(vmem_limit_bytes=2 << 20),
        name="write_out",
    )(*arrays)


def local(n_exc, n_space, *args):
    (adj_e, adj_h, adj_j, fwd_e, inv_eps, drude, neighbor, design, ports, profile) = args
    own_rows = LAYER // n_exc
    f32 = jnp.float32
    anywhere = pl.BlockSpec(memory_space=pltpu.HBM)
    in_vmem = pl.BlockSpec(memory_space=pltpu.VMEM)
    new_e, new_h, grad_eps, grad_drude = pl.pallas_call(
        functools.partial(kernel, n_exc, n_space),
        out_shape=(
            jax.ShapeDtypeStruct(adj_e.shape, f32),
            jax.ShapeDtypeStruct(adj_h.shape, f32),
            jax.ShapeDtypeStruct((own_rows, 64), f32),
            jax.ShapeDtypeStruct((own_rows, 64), f32),
        ),
        in_specs=[anywhere] * 12,
        out_specs=(anywhere, anywhere, in_vmem, in_vmem),
        scratch_shapes=[
            pltpu.VMEM((2, 192, LAYER), f32),
            pltpu.VMEM((2, 192, LAYER), f32),
            pltpu.VMEM((2, 192, LAYER), f32),
            pltpu.VMEM((STEPS, 2, 192, LAYER), f32),
            pltpu.VMEM((STEPS, 2, 192, LAYER), f32),
            pltpu.VMEM((2, 2, 192, LAYER), f32),
            pltpu.VMEM((2, 192, LAYER), f32),
            pltpu.VMEM((2, 192, LAYER), f32),
            pltpu.VMEM((2, 2, LAYER, LAYER), f32),
            pltpu.VMEM((4, 192, LAYER), f32),
            pltpu.VMEM((2, STEPS + 1, 192, LAYER), jnp.bfloat16),
            pltpu.VMEM((2, 64, LAYER), f32),
            pltpu.VMEM((2, 64, LAYER), f32),
            pltpu.VMEM((4, 64, LAYER), f32),
            pltpu.VMEM((6, 2 * LAYER), jnp.int32),
            pltpu.VMEM((1, 2 * LAYER), jnp.int32),
            pltpu.VMEM((1, LAYER), jnp.int32),
            pltpu.VMEM((192, LAYER), f32),
            pltpu.VMEM((384, 192), jnp.bfloat16),
            pltpu.VMEM((2, 192, 96), jnp.bfloat16),
            pltpu.VMEM((STEPS // 2, 4, 2, 32, LAYER), f32),
            pltpu.VMEM((STEPS // 2, 4, 2, 32, LAYER), f32),
            pltpu.VMEM((2, 64, LAYER), f32),
            pltpu.VMEM((2, 6, LAYER), jnp.int32),
            pltpu.VMEM((LAYER, LAYER), f32),
            pltpu.VMEM((n_exc, own_rows, LAYER), f32),
            pltpu.SemaphoreType.DMA((24,)),
            pltpu.SemaphoreType.DMA((STEPS // 2, 4, 2)),
            pltpu.SemaphoreType.DMA((STEPS // 2, 4, 2)),
            pltpu.SemaphoreType.DMA((2, 2)),
            pltpu.SemaphoreType.DMA((2, 2)),
            pltpu.SemaphoreType.DMA((n_exc,)),
            pltpu.SemaphoreType.DMA((n_exc,)),
            pltpu.SemaphoreType.DMA((4,)),
        ],
        compiler_params=pltpu.CompilerParams(
            collective_id=0, has_side_effects=True, vmem_limit_bytes=16 << 20
        ),
        name="adjoint_steps",
    )(
        *[pltpu.with_memory_space_constraint(x, pltpu.HBM) for x in (adj_e, adj_h, adj_j, fwd_e, inv_eps, drude, neighbor, design.reshape(1, 2 * LAYER), ports, profile, jnp.asarray(split_table()), jnp.asarray(split_faces()))]
    )
    new_e, new_h, grad_eps, grad_drude = write(new_e, new_h, grad_eps, grad_drude)
    return new_e, new_h, grad_eps.T, grad_drude.T


def solution(mesh):
    return jax.shard_map(
        functools.partial(local, mesh.shape["exc"], mesh.shape["space"]),
        mesh=mesh,
        in_specs=(
            P("exc", None, "space"),
            P("exc", None, "space"),
            P("exc", None, "space"),
            P("exc", None, None, "space"),
            P(None, "space"),
            P(None, "space"),
            P(None, "space"),
            P("space"),
            P("exc", "space"),
            P("exc", None, "space"),
        ),
        out_specs=(
            P("exc", None, "space"),
            P("exc", None, "space"),
            P(None, ("space", "exc")),
            P(None, ("space", "exc")),
        ),
        check_vma=False,
    )
```

```python
import functools

import jax
import jax.numpy as jnp
import ml_dtypes
import numpy as np
from jax import lax
from jax.experimental import pallas as pl
from jax.experimental.pallas import tpu as pltpu
from jax.sharding import PartitionSpec as P

STEPS = 4
LAYER = 128
TIME_STEP = 0.025
DAMPING = 0.5
GAIN = 6.0 * TIME_STEP
MESH = pl.DeviceIdType.MESH


def operator_table():
    points = np.array([-1.0, -1.0 / np.sqrt(5.0), 1.0 / np.sqrt(5.0), 1.0])
    barycentric = np.array(
        [1.0 / np.prod([points[j] - points[k] for k in range(4) if k != j]) for j in range(4)]
    )
    deriv = np.zeros((4, 4))
    for row in range(4):
        for column in range(4):
            if row != column:
                deriv[row, column] = (
                    barycentric[column] / barycentric[row] / (points[row] - points[column])
                )
        deriv[row, row] = -np.sum(deriv[row])
    identity = np.eye(4)
    along_x = 2.0 * np.kron(np.kron(deriv, identity), identity)
    along_y = 2.0 * np.kron(np.kron(identity, deriv), identity)
    along_z = 2.0 * np.kron(np.kron(identity, identity), deriv)
    curl = np.zeros((192, 192))
    curl[0:64, 64:128] = -along_z
    curl[0:64, 128:192] = along_y
    curl[64:128, 0:64] = along_z
    curl[64:128, 128:192] = -along_x
    curl[128:192, 0:64] = -along_y
    curl[128:192, 64:128] = along_x
    numbers = np.arange(64).reshape(4, 4, 4)
    faces = [
        numbers[0].ravel(),
        numbers[3].ravel(),
        numbers[:, 0].ravel(),
        numbers[:, 3].ravel(),
        numbers[:, :, 0].ravel(),
        numbers[:, :, 3].ravel(),
    ]
    inner = np.zeros((192, 192))
    for face in range(6):
        direction = face // 2
        sign = 1.0 if face % 2 else -1.0
        for component in range(3):
            for other in range(3):
                parity = (component - direction) * (direction - other) * (other - component) / 2.0
                for node in faces[face]:
                    inner[component * 64 + node, other * 64 + node] += sign * parity
    return inner - curl / 6.0


def split_table():
    table = operator_table()
    high = table.astype(ml_dtypes.bfloat16)
    low = (table - high.astype(np.float64)).astype(ml_dtypes.bfloat16)
    return np.concatenate([high, low], axis=0)


def split_faces():
    table = split_table()
    tables = []
    for start in (0, 48):
        rows = np.concatenate([np.arange(64, 80), np.arange(128, 144)]) + start
        high, low = table[0:192, rows], table[192:384, rows]
        tables.append(np.concatenate([high, low, high], axis=1))
    return np.stack(tables)


def halves(value):
    high = value.astype(jnp.bfloat16)
    low = (value - high.astype(jnp.float32)).astype(jnp.bfloat16)
    return high, low


def pick(value, index):
    index = jnp.broadcast_to(index, value.shape)
    return jnp.take_along_axis(value, index, axis=1, mode="promise_in_bounds")


def rows_of(ref, layer, start):
    return jnp.concatenate(
        [ref[layer, 64 + start : 80 + start], ref[layer, 128 + start : 144 + start]], axis=0
    )


def turn(trace, sign):
    return jnp.concatenate([sign * trace[16:32], -sign * trace[0:16]], axis=0)


def add_rows(ref, layer, start, value):
    ref[layer, 64 + start : 80 + start] += value[0:16]
    ref[layer, 128 + start : 144 + start] += value[16:32]


FAR_FIRST = (10, 6, 14, 2, 9, 11, 8, 5, 7, 13, 15, 1, 3, 4, 12)
MINE = (0, 48)
THEIRS = (48, 0)
SIGN = (-1.0, 1.0)


def kernel(
    n_exc,
    n_space,
    adj_e,
    adj_h,
    adj_j,
    fwd_e,
    inv_eps,
    drude,
    neighbor,
    design,
    ports,
    profile,
    table,
    face_table,
    out_e,
    out_h,
    out_eps,
    out_drude,
    e_ref,
    h_ref,
    j_ref,
    level_e,
    level_j,
    change_ref,
    late_ref,
    s_ref,
    z_ref,
    de_ref,
    f_ref,
    v_ref,
    w_ref,
    kick_ref,
    nb_ref,
    dm_ref,
    pe_ref,
    pp_ref,
    tb_ref,
    fb_ref,
    send_t,
    recv_t,
    recv_v,
    recv_nb,
    sums,
    parts,
    load_sem,
    send_sem,
    recv_sem,
    once_send_sem,
    once_recv_sem,
    part_send_sem,
    part_recv_sem,
    store_sem,
):
    me_exc = lax.axis_index("exc")
    me_space = lax.axis_index("space")
    left = lax.rem(me_space + n_space - 1, n_space)
    right = lax.rem(me_space + 1, n_space)
    own_rows = LAYER // n_exc
    f32 = jnp.float32

    barrier = pltpu.get_barrier_semaphore()
    has = (me_space > 0, me_space < n_space - 1)
    for side, peer in enumerate((left, right)):

        @pl.when(has[side])
        def _():
            pl.semaphore_signal(barrier, inc=1, device_id={"space": peer}, device_id_type=MESH)


    loads = []

    def load(src, dst):
        copy = pltpu.make_async_copy(src, dst, load_sem.at[len(loads)])
        copy.start()
        loads.append(copy)
        return copy

    def load_layers(src, dst):
        return [load(src.at[..., pl.ds(n * LAYER, LAYER)], dst.at[n]) for n in range(2)]

    got_nb = load(neighbor, nb_ref)
    got_e = load_layers(adj_e.at[0], e_ref)
    got_tb = load(table, tb_ref)
    got_h = load_layers(adj_h.at[0], h_ref)
    got_v = load_layers(inv_eps, v_ref)
    got_w = load_layers(drude, w_ref)
    got_j = load_layers(adj_j.at[0], j_ref)
    got_pe = load(ports, pe_ref)
    got_pp = load(profile.at[0], pp_ref)
    got_fb = load(face_table, fb_ref)
    got_f = load_layers(fwd_e.at[0], f_ref)
    got_dm = load(design, dm_ref)

    for hop in range(1, n_exc):
        peer = lax.rem(me_exc + hop, n_exc)
        pl.semaphore_signal(barrier, inc=1, device_id={"exc": peer}, device_id_type=MESH)

    sublane = lax.broadcasted_iota(jnp.int32, (8, LAYER), 0)
    lower = sublane < 4
    first_k = (sublane & 3) == 0
    last_k = (sublane & 3) == 3

    z_ref[...] = jnp.zeros(z_ref.shape, f32)
    for side in range(2):

        @pl.when(jnp.logical_not(has[side]))
        def _():
            for window in range(STEPS // 2):
                for kind in range(4):
                    recv_t[window, kind, side] = jnp.zeros((32, LAYER), f32)
            recv_v[side] = jnp.zeros((64, LAYER), f32)
            recv_nb[side] = jnp.zeros((6, LAYER), jnp.int32)


    got_nb.wait()
    table_nb = nb_ref[...]
    place = table_nb & (LAYER - 1)

    def face(number, layer):
        return place[number : number + 1, layer * LAYER : (layer + 1) * LAYER]

    def inside(number, layer):
        cut = table_nb[number : number + 1, layer * LAYER : (layer + 1) * LAYER]
        return (cut >= 0).astype(f32)

    edge_y = [jnp.where(lower, face(3, n), face(2, n)) for n in range(2)]
    edge_z = [jnp.where(first_k, face(5, n), face(4, n)) for n in range(2)]
    along_y = [jnp.concatenate([index] * 8, axis=0) for index in edge_y]
    low_z = [face(4, n) for n in range(2)]
    high_z = [face(5, n) for n in range(2)]
    between = [face(1, 0), face(0, 1)]
    beyond = [face(0, 0), face(1, 1)]
    exists = [inside(0, 0), inside(1, 1)]

    def product(field):
        high, low = halves(field)
        whole = jnp.dot(tb_ref[...], high, preferred_element_type=f32)
        rest = jnp.dot(tb_ref[0:192, :], low, preferred_element_type=f32)
        return whole[0:192] + (whole[192:384] + rest)

    calls = []

    def local_flux(field_ref):
        total = product(jnp.concatenate([field_ref[0], field_ref[1]], axis=1))
        zeros = jnp.zeros((48, LAYER), f32)
        slot = len(calls) % 2
        calls.append(slot)
        result = []
        for n in range(2):
            far = pick(field_ref[n, pl.ds(0, 32, stride=4), :], high_z[n])
            z_ref[slot, n, pl.ds(3, 32, stride=4), :] = jnp.concatenate(
                [far[16:32], -far[0:16]], axis=0
            )
            near = pick(field_ref[n, pl.ds(3, 32, stride=4), :], low_z[n])
            z_ref[slot, n, pl.ds(0, 32, stride=4), :] = jnp.concatenate(
                [-near[16:32], near[0:16]], axis=0
            )
            own = field_ref[n].reshape(3, 4, 2, 8, LAYER)
            edge = jnp.concatenate(
                [
                    jnp.where(lower, own[0, :, 0], own[0, :, 1]),
                    jnp.where(lower, own[2, :, 0], own[2, :, 1]),
                ],
                axis=0,
            )
            outer = pick(edge.reshape(64, LAYER), along_y[n]).reshape(8, 8, LAYER)
            outer = pltpu.roll(outer, 4, 1)
            zero = jnp.zeros((4, 8, LAYER), f32)
            o_x, o_z = outer[0:4], outer[4:8]
            to_x = jnp.stack([jnp.where(lower, o_z, zero), jnp.where(lower, zero, -o_z)], axis=1)
            to_z = jnp.stack([jnp.where(lower, -o_x, zero), jnp.where(lower, zero, o_x)], axis=1)
            if n == 0:
                side = turn(pick(rows_of(field_ref, 1, 0), between[0]), 1.0)
                to_y = jnp.concatenate([zeros, side[0:16]], axis=0)
                to_z2 = jnp.concatenate([zeros, side[16:32]], axis=0)
            else:
                side = turn(pick(rows_of(field_ref, 0, 48), between[1]), -1.0)
                to_y = jnp.concatenate([side[0:16], zeros], axis=0)
                to_z2 = jnp.concatenate([side[16:32], zeros], axis=0)
            extra = jnp.concatenate(
                [
                    z_ref[slot, n, 0:64] + to_x.reshape(64, LAYER),
                    z_ref[slot, n, 64:128] + to_y,
                    to_z.reshape(64, LAYER) + to_z2,
                ],
                axis=0,
            )
            result.append(total[:, n * LAYER : (n + 1) * LAYER] + extra)
        return result

    def from_y(rows, index):
        outer = pltpu.roll(pick(jnp.where(lower, rows[0:8], rows[8:16]), index), 4, 0)
        zero = jnp.zeros((8, LAYER), f32)
        return jnp.concatenate(
            [jnp.where(lower, outer, zero), jnp.where(lower, zero, -outer)], axis=0
        )

    def from_z(rows, index):
        parts_z = []
        zero = jnp.zeros((8, LAYER), f32)
        for half in (rows[0:8], rows[8:16]):
            outer = pick(half, index)
            parts_z.append(
                jnp.where(last_k, pltpu.roll(outer, 3, 0), zero)
                - jnp.where(first_k, pltpu.roll(outer, 5, 0), zero)
            )
        return jnp.concatenate(parts_z, axis=0)

    def remote(src, dst, sems, side):
        copy = pltpu.make_async_remote_copy(
            src_ref=src,
            dst_ref=dst,
            send_sem=sems[0],
            recv_sem=sems[1],
            device_id={"space": (left, right)[side]},
            device_id_type=MESH,
        )

        @pl.when(has[side])
        def _():
            copy.start()

        return copy, side

    def arrive(copies):
        for copy, side in copies:
            pl.when(has[1 - side])(copy.wait_recv)

    def leave(copies):
        for copy, side in copies:
            pl.when(has[side])(copy.wait_send)

    sent = []

    def keep_trace(window, kind, ref):
        for side in range(2):
            send_t[window, kind, side] = rows_of(ref, side, MINE[side])

    def send_trace(window, kind):
        copies = []
        for side in range(2):
            copies.append(
                remote(
                    send_t.at[window, kind, side],
                    recv_t.at[window, kind, 1 - side],
                    (send_sem.at[window, kind, side], recv_sem.at[window, kind, 1 - side]),
                    side,
                )
            )
        sent.extend(copies)
        return copies

    sens = [[jnp.zeros((64, LAYER), f32)] * 2 for _ in range(2)]

    def add(kind, n, field, weight):
        term = (field * weight).reshape(3, 64, LAYER)
        sens[kind][n] = sens[kind][n] + (term[0] + term[1] + term[2])

    def change_of(n, step):
        return f_ref[n, step + 1].astype(f32) - f_ref[n, step].astype(f32)

    def add_eps(step):
        for n in range(2):
            add(0, n, level_e[step, n], change_of(n, step))

    def add_drude(step):
        for n in range(2):
            add(1, n, level_j[step, n], f_ref[n, step].astype(f32))

    def drive(step):
        for n in range(2):
            electric = (level_e[step - 1, n] if step else e_ref[n]).reshape(3, 64, LAYER)
            current = level_j[step - 1, n] if step else j_ref[n]
            current = (1.0 - TIME_STEP * DAMPING) * current.reshape(3, 64, LAYER)
            current = current + w_ref[n] * electric
            level_j[step, n] = current.reshape(192, LAYER)
            push = v_ref[n] * (current + s_ref[n].reshape(3, 64, LAYER))
            e_ref[n] = (electric - push).reshape(192, LAYER)

    def gather_pixels(stacked):
        pixel = lax.broadcasted_iota(jnp.int32, (LAYER, 2 * LAYER), 0)
        members = ((dm_ref[...] & (LAYER - 1)) == pixel).astype(jnp.bfloat16)
        high, low = halves(stacked)
        contract = (((1,), (1,)), ((), ()))
        return lax.dot_general(
            members, high, contract, preferred_element_type=f32
        ) + lax.dot_general(members, low, contract, preferred_element_type=f32)

    def kick(n, flux):
        return (kick_ref[n] * flux.reshape(3, 64, LAYER)).reshape(192, LAYER)

    ghost_y, ghost_z = [None, None], [None, None]

    for copy in got_e:
        copy.wait()

    for window in range(STEPS // 2):
        step = 2 * window
        field = e_ref if window == 0 else level_e.at[step - 1]
        keep_trace(window, 0, field)
        if window > 0:
            e0 = send_trace(window, 0)
        if window == 0:
            got_tb.wait()
        flux = local_flux(field)
        if window == 0:
            for copy in got_h:
                copy.wait()
        for n in range(2):
            h_ref[n] = h_ref[n] + GAIN * flux[n]
        keep_trace(window, 1, h_ref)
        if window == 0:
            arrivals = has[0].astype(jnp.int32) + has[1].astype(jnp.int32)
            pl.semaphore_wait(barrier, arrivals + (n_exc - 1))
            e0 = send_trace(window, 0)
        h1 = send_trace(window, 1)
        if window == 0:
            once = []
            for side in range(2):
                lanes = pl.ds(side * LAYER, LAYER)
                for at, (src, dst) in enumerate(((inv_eps, recv_v), (neighbor, recv_nb))):
                    once.append(
                        remote(
                            src.at[:, lanes],
                            dst.at[1 - side],
                            (once_send_sem.at[at, side], once_recv_sem.at[at, 1 - side]),
                            side,
                        )
                    )

        if window == 0:
            for copy in got_w + got_v + got_j + [got_pe, got_pp]:
                copy.wait()
            element = lax.broadcasted_iota(jnp.int32, (2 * LAYER, LAYER), 0)
            chosen = ((pe_ref[...] & (2 * LAYER - 1)) == element).astype(jnp.bfloat16)
            high, low = halves(pp_ref[...])
            contract = (((1,), (1,)), ((), ()))
            source = lax.dot_general(
                high, chosen, contract, preferred_element_type=f32
            ) + lax.dot_general(low, chosen, contract, preferred_element_type=f32)
            for n in range(2):
                s_ref[n] = source[:, n * LAYER : (n + 1) * LAYER]
                kick_ref[n] = GAIN * v_ref[n]
                v_ref[n] = TIME_STEP * v_ref[n]
                w_ref[n] = TIME_STEP * w_ref[n]
        drive(step)
        flux = local_flux(h_ref)
        for n in range(2):
            e_ref[n] = e_ref[n] - kick(n, flux[n])
        keep_trace(window, 2, e_ref)
        e1 = send_trace(window, 2)
        flux = local_flux(e_ref)
        for n in range(2):
            h_ref[n] = h_ref[n] + GAIN * flux[n]
        keep_trace(window, 3, h_ref)
        h2 = send_trace(window, 3)

        if window == 0:
            for copy in got_f + [got_fb, got_dm]:
                copy.wait()
        add_drude(step)
        if step + 2 < STEPS:
            pass
        else:
            add_eps(step - 2)
            add_eps(step - 1)
            add_drude(step - 1)
            for n in range(2):
                for at in range(2):
                    change_ref[at, n] = change_of(n, step + at)
                late_ref[n] = f_ref[n, step + 1].astype(f32)
        arrive(e0)
        mine_dh, their_dh = [], []
        for side in range(2):
            sign = SIGN[side]
            outer = pick(recv_t[window, 0, side], beyond[side]) * exists[side]
            mine_dh.append(turn(outer, GAIN * sign))
            their_dh.append(turn(send_t[window, 0, side], -GAIN * sign))
        pairs = ((mine_dh[0], their_dh[1]), (mine_dh[1], their_dh[0]))
        spread = []
        for at in range(2):
            high, low = halves(jnp.concatenate(pairs[at], axis=1))
            spread.append(
                jnp.dot(
                    fb_ref[at],
                    jnp.concatenate([high, high, low], axis=0),
                    preferred_element_type=f32,
                )
            )

        def respond(side, ghost, across):
            layer = 2 + side if ghost else side
            start = THEIRS[side] if ghost else MINE[side]
            change = their_dh[side] if ghost else mine_dh[side]
            index_y = ghost_y[side] if ghost else edge_y[side]
            index_z = ghost_z[side] if ghost else edge_z[side]
            if ghost:
                out = spread[1 - side][:, LAYER : 2 * LAYER]
            else:
                out = spread[side][:, 0:LAYER]
            edge = from_y(change[16:32], index_y) + from_z(change[0:16], index_z)

            def with_face(rows, extra):
                end = start + 16
                middle = rows[start:end] + extra
                if start == 0:
                    return jnp.concatenate([middle, rows[end:64]], axis=0)
                return jnp.concatenate([rows[0:start], middle], axis=0)

            speed = kick_ref[layer]
            de_ref[layer, 0:64] = -speed * with_face(out[0:64], edge)
            de_ref[layer, 64:128] = -speed * with_face(out[64:128], across[0:16])
            de_ref[layer, 128:192] = -speed * with_face(out[128:192], across[16:32])

        def respond_ghosts():
            for side in range(2):
                across = send_t[window, 1, side] + mine_dh[side]
                respond(side, True, turn(across, -SIGN[side]))

        if window > 0:
            respond_ghosts()
        arrive(h1)
        for side in range(2):
            across = (pick(recv_t[window, 1, side], beyond[side]) + their_dh[side]) * exists[side]
            respond(side, False, turn(across, SIGN[side]))
        for n in range(2):
            level_e[step, n] = e_ref[n] + de_ref[n]
            add_rows(h_ref, n, MINE[n], mine_dh[n])
        flux = local_flux(de_ref)
        for n in range(2):
            h_ref[n] = h_ref[n] + GAIN * flux[n]

        if window == 0:
            arrive(once)
            for side in range(2):
                kick_ref[2 + side] = GAIN * pick(recv_v[side], beyond[side])
                far = recv_nb[side] & (LAYER - 1)
                back = jnp.broadcast_to(far[1 - side : 2 - side], (8, LAYER))

                def through(number):
                    rows = jnp.broadcast_to(far[number : number + 1], (8, LAYER))
                    return pick(back, pick(rows, beyond[side]))

                ghost_y[side] = jnp.where(lower, through(3), through(2))
                ghost_z[side] = jnp.where(first_k, through(5), through(4))
            respond_ghosts()

        def their_second():
            high, low = halves(jnp.concatenate([de_ref[2], de_ref[3]], axis=1))
            cuts = [tb_ref[at : at + 16, :] for at in (112, 176, 64, 128)]
            lows = [tb_ref[192 + at : 208 + at, :] for at in (112, 176, 64, 128)]
            whole = jnp.dot(jnp.concatenate(cuts + lows, axis=0), high, preferred_element_type=f32)
            rest = jnp.dot(jnp.concatenate(cuts, axis=0), low, preferred_element_type=f32)
            near = whole[0:64] + (whole[64:128] + rest)
            result = []
            for side in range(2):
                start = THEIRS[side]
                own = de_ref[2 + side, start : start + 16]
                edge = jnp.concatenate(
                    [-from_z(own, ghost_z[side]), -from_y(own, ghost_y[side])], axis=0
                )
                across = turn(rows_of(level_e.at[step], side, MINE[side]), -SIGN[side])
                lanes = slice(side * LAYER, (side + 1) * LAYER)
                at = slice(32 * side, 32 * side + 32)
                result.append(their_dh[side] + GAIN * (near[at, lanes] + edge + across))
            return result

        arrive(e1)
        for side in range(2):
            outer = pick(recv_t[window, 2, side], beyond[side])
            outer = (outer + rows_of(de_ref, 2 + side, THEIRS[side])) * exists[side]
            add_rows(h_ref, side, MINE[side], turn(outer, GAIN * SIGN[side]))
        drive(step + 1)
        flux = local_flux(h_ref)
        for n in range(2):
            level_e[step + 1, n] = e_ref[n] - kick(n, flux[n])
        if step + 2 == STEPS:
            for n in range(2):
                add(0, n, level_e[step, n], change_ref[0, n])
                add(1, n, level_j[step + 1, n], late_ref[n])
            sums[...] = gather_pixels(
                jnp.concatenate(
                    [jnp.concatenate(sens[0], axis=1), jnp.concatenate(sens[1], axis=1)], axis=0
                )
            )
        their_dh2 = their_second()
        arrive(h2)
        for side in range(2):
            outer = pick(recv_t[window, 3, side], beyond[side])
            outer = turn((outer + their_dh2[side]) * exists[side], -SIGN[side])
            speed = kick_ref[side, MINE[side] : MINE[side] + 16]
            add_rows(
                level_e.at[step + 1],
                side,
                MINE[side],
                jnp.concatenate([speed * outer[0:16], speed * outer[16:32]], axis=0),
            )

    sens[0] = [jnp.zeros((64, LAYER), f32)] * 2
    for n in range(2):
        add(0, n, level_e[STEPS - 1, n], change_ref[1, n])
    sums[:, 0:64] += gather_pixels(jnp.concatenate(sens[0], axis=1))
    part_copies = {}
    for hop in FAR_FIRST if n_exc == 16 else range(1, n_exc):
        peer = lax.rem(me_exc + hop, n_exc)
        start = pl.multiple_of(peer * own_rows, own_rows)
        copy = pltpu.make_async_remote_copy(
            src_ref=sums.at[pl.ds(start, own_rows)],
            dst_ref=parts.at[hop],
            send_sem=part_send_sem.at[hop],
            recv_sem=part_recv_sem.at[hop],
            device_id={"exc": peer},
            device_id_type=MESH,
        )
        copy.start()
        part_copies[hop] = copy
    stores = []
    for n in range(2):
        lanes = pl.ds(n * LAYER, LAYER)
        for at, (src, dst) in enumerate(((h_ref, out_h), (level_e.at[STEPS - 1], out_e))):
            copy = pltpu.make_async_copy(
                src.at[n], dst.at[0, :, lanes], store_sem.at[2 * at + n]
            )
            copy.start()
            stores.append(copy)
    leave(sent + once)
    total = sums[pl.ds(pl.multiple_of(me_exc * own_rows, own_rows), own_rows)]
    for hop in range(1, n_exc):
        part_copies[hop].wait_recv()
        total = total + parts[hop]
    total = total * (1.0 / n_exc)
    out_eps[...] = total[:, 0:64]
    out_drude[...] = total[:, 64:128]
    for copy in part_copies.values():
        copy.wait_send()
    for copy in stores:
        copy.wait()


def write_kernel(e_in, h_in, a_in, b_in, e_out, h_out, a_out, b_out, sem):
    copies = [
        pltpu.make_async_copy(src, dst, sem.at[at])
        for at, (src, dst) in enumerate(
            ((e_in, e_out), (h_in, h_out), (a_in, a_out), (b_in, b_out))
        )
    ]
    for copy in copies:
        copy.start()
    for copy in copies:
        copy.wait()


def write(*arrays):
    spec = pl.BlockSpec(memory_space=pltpu.HBM)
    return pl.pallas_call(
        write_kernel,
        out_shape=tuple(jax.ShapeDtypeStruct(a.shape, a.dtype) for a in arrays),
        in_specs=[pl.BlockSpec(memory_space=pltpu.VMEM)] * 4,
        out_specs=(spec,) * 4,
        scratch_shapes=[pltpu.SemaphoreType.DMA((4,))],
        compiler_params=pltpu.CompilerParams(vmem_limit_bytes=2 << 20),
        name="write_out",
    )(*arrays)


def local(n_exc, n_space, *args):
    (adj_e, adj_h, adj_j, fwd_e, inv_eps, drude, neighbor, design, ports, profile) = args
    own_rows = LAYER // n_exc
    f32 = jnp.float32
    anywhere = pl.BlockSpec(memory_space=pltpu.HBM)
    in_vmem = pl.BlockSpec(memory_space=pltpu.VMEM)
    new_e, new_h, grad_eps, grad_drude = pl.pallas_call(
        functools.partial(kernel, n_exc, n_space),
        out_shape=(
            jax.ShapeDtypeStruct(adj_e.shape, f32),
            jax.ShapeDtypeStruct(adj_h.shape, f32),
            jax.ShapeDtypeStruct((own_rows, 64), f32),
            jax.ShapeDtypeStruct((own_rows, 64), f32),
        ),
        in_specs=[anywhere] * 12,
        out_specs=(anywhere, anywhere, in_vmem, in_vmem),
        scratch_shapes=[
            pltpu.VMEM((2, 192, LAYER), f32),
            pltpu.VMEM((2, 192, LAYER), f32),
            pltpu.VMEM((2, 192, LAYER), f32),
            pltpu.VMEM((STEPS, 2, 192, LAYER), f32),
            pltpu.VMEM((STEPS, 2, 192, LAYER), f32),
            pltpu.VMEM((2, 2, 192, LAYER), f32),
            pltpu.VMEM((2, 192, LAYER), f32),
            pltpu.VMEM((2, 192, LAYER), f32),
            pltpu.VMEM((2, 2, LAYER, LAYER), f32),
            pltpu.VMEM((4, 192, LAYER), f32),
            pltpu.VMEM((2, STEPS + 1, 192, LAYER), jnp.bfloat16),
            pltpu.VMEM((2, 64, LAYER), f32),
            pltpu.VMEM((2, 64, LAYER), f32),
            pltpu.VMEM((4, 64, LAYER), f32),
            pltpu.VMEM((6, 2 * LAYER), jnp.int32),
            pltpu.VMEM((1, 2 * LAYER), jnp.int32),
            pltpu.VMEM((1, LAYER), jnp.int32),
            pltpu.VMEM((192, LAYER), f32),
            pltpu.VMEM((384, 192), jnp.bfloat16),
            pltpu.VMEM((2, 192, 96), jnp.bfloat16),
            pltpu.VMEM((STEPS // 2, 4, 2, 32, LAYER), f32),
            pltpu.VMEM((STEPS // 2, 4, 2, 32, LAYER), f32),
            pltpu.VMEM((2, 64, LAYER), f32),
            pltpu.VMEM((2, 6, LAYER), jnp.int32),
            pltpu.VMEM((LAYER, LAYER), f32),
            pltpu.VMEM((n_exc, own_rows, LAYER), f32),
            pltpu.SemaphoreType.DMA((24,)),
            pltpu.SemaphoreType.DMA((STEPS // 2, 4, 2)),
            pltpu.SemaphoreType.DMA((STEPS // 2, 4, 2)),
            pltpu.SemaphoreType.DMA((2, 2)),
            pltpu.SemaphoreType.DMA((2, 2)),
            pltpu.SemaphoreType.DMA((n_exc,)),
            pltpu.SemaphoreType.DMA((n_exc,)),
            pltpu.SemaphoreType.DMA((4,)),
        ],
        compiler_params=pltpu.CompilerParams(
            collective_id=0, has_side_effects=True, vmem_limit_bytes=16 << 20
        ),
        name="adjoint_steps",
    )(
        *[pltpu.with_memory_space_constraint(x, pltpu.HBM) for x in (adj_e, adj_h, adj_j, fwd_e, inv_eps, drude, neighbor, design.reshape(1, 2 * LAYER), ports, profile, jnp.asarray(split_table()), jnp.asarray(split_faces()))]
    )
    new_e, new_h, grad_eps, grad_drude = write(new_e, new_h, grad_eps, grad_drude)
    return new_e, new_h, grad_eps.T, grad_drude.T


def solution(mesh):
    return jax.shard_map(
        functools.partial(local, mesh.shape["exc"], mesh.shape["space"]),
        mesh=mesh,
        in_specs=(
            P("exc", None, "space"),
            P("exc", None, "space"),
            P("exc", None, "space"),
            P("exc", None, None, "space"),
            P(None, "space"),
            P(None, "space"),
            P(None, "space"),
            P("space"),
            P("exc", "space"),
            P("exc", None, "space"),
        ),
        out_specs=(
            P("exc", None, "space"),
            P("exc", None, "space"),
            P(None, ("space", "exc")),
            P(None, ("space", "exc")),
        ),
        check_vma=False,
    )
```

```python
import functools

import jax
import jax.numpy as jnp
import ml_dtypes
import numpy as np
from jax import lax
from jax.experimental import pallas as pl
from jax.experimental.pallas import tpu as pltpu
from jax.sharding import PartitionSpec as P

STEPS = 4
LAYER = 128
TIME_STEP = 0.025
DAMPING = 0.5
GAIN = 6.0 * TIME_STEP
MESH = pl.DeviceIdType.MESH


def operator_table():
    points = np.array([-1.0, -1.0 / np.sqrt(5.0), 1.0 / np.sqrt(5.0), 1.0])
    barycentric = np.array(
        [1.0 / np.prod([points[j] - points[k] for k in range(4) if k != j]) for j in range(4)]
    )
    deriv = np.zeros((4, 4))
    for row in range(4):
        for column in range(4):
            if row != column:
                deriv[row, column] = (
                    barycentric[column] / barycentric[row] / (points[row] - points[column])
                )
        deriv[row, row] = -np.sum(deriv[row])
    identity = np.eye(4)
    along_x = 2.0 * np.kron(np.kron(deriv, identity), identity)
    along_y = 2.0 * np.kron(np.kron(identity, deriv), identity)
    along_z = 2.0 * np.kron(np.kron(identity, identity), deriv)
    curl = np.zeros((192, 192))
    curl[0:64, 64:128] = -along_z
    curl[0:64, 128:192] = along_y
    curl[64:128, 0:64] = along_z
    curl[64:128, 128:192] = -along_x
    curl[128:192, 0:64] = -along_y
    curl[128:192, 64:128] = along_x
    numbers = np.arange(64).reshape(4, 4, 4)
    faces = [
        numbers[0].ravel(),
        numbers[3].ravel(),
        numbers[:, 0].ravel(),
        numbers[:, 3].ravel(),
        numbers[:, :, 0].ravel(),
        numbers[:, :, 3].ravel(),
    ]
    inner = np.zeros((192, 192))
    for face in range(6):
        direction = face // 2
        sign = 1.0 if face % 2 else -1.0
        for component in range(3):
            for other in range(3):
                parity = (component - direction) * (direction - other) * (other - component) / 2.0
                for node in faces[face]:
                    inner[component * 64 + node, other * 64 + node] += sign * parity
    return inner - curl / 6.0


def split_table():
    table = operator_table()
    high = table.astype(ml_dtypes.bfloat16)
    low = (table - high.astype(np.float64)).astype(ml_dtypes.bfloat16)
    return np.concatenate([high, low], axis=0)


def split_faces():
    table = split_table()
    tables = []
    for start in (0, 48):
        rows = np.concatenate([np.arange(64, 80), np.arange(128, 144)]) + start
        high, low = table[0:192, rows], table[192:384, rows]
        tables.append(np.concatenate([high, low, high], axis=1))
    return np.stack(tables)


def halves(value):
    high = value.astype(jnp.bfloat16)
    low = (value - high.astype(jnp.float32)).astype(jnp.bfloat16)
    return high, low


def pick(value, index):
    index = jnp.broadcast_to(index, value.shape)
    return jnp.take_along_axis(value, index, axis=1, mode="promise_in_bounds")


def rows_of(ref, layer, start):
    return jnp.concatenate(
        [ref[layer, 64 + start : 80 + start], ref[layer, 128 + start : 144 + start]], axis=0
    )


def turn(trace, sign):
    return jnp.concatenate([sign * trace[16:32], -sign * trace[0:16]], axis=0)


def add_rows(ref, layer, start, value):
    ref[layer, 64 + start : 80 + start] += value[0:16]
    ref[layer, 128 + start : 144 + start] += value[16:32]


FAR_FIRST = (10, 6, 14, 2, 9, 11, 8, 5, 7, 13, 15, 1, 3, 4, 12)
MINE = (0, 48)
THEIRS = (48, 0)
SIGN = (-1.0, 1.0)


def kernel(
    n_exc,
    n_space,
    adj_e,
    adj_h,
    adj_j,
    fwd_e,
    inv_eps,
    drude,
    neighbor,
    design,
    ports,
    profile,
    table,
    face_table,
    out_e,
    out_h,
    out_eps,
    out_drude,
    e_ref,
    h_ref,
    j_ref,
    level_e,
    level_j,
    change_ref,
    late_ref,
    s_ref,
    z_ref,
    de_ref,
    f_ref,
    v_ref,
    w_ref,
    kick_ref,
    nb_ref,
    dm_ref,
    pe_ref,
    pp_ref,
    tb_ref,
    fb_ref,
    send_t,
    recv_t,
    recv_v,
    recv_nb,
    sums,
    parts,
    load_sem,
    send_sem,
    recv_sem,
    once_send_sem,
    once_recv_sem,
    part_send_sem,
    part_recv_sem,
    store_sem,
):
    me_exc = lax.axis_index("exc")
    me_space = lax.axis_index("space")
    left = lax.rem(me_space + n_space - 1, n_space)
    right = lax.rem(me_space + 1, n_space)
    own_rows = LAYER // n_exc
    f32 = jnp.float32

    def around(hop):
        if n_exc & (n_exc - 1) == 0:
            return (me_exc + hop) & (n_exc - 1)
        return lax.rem(me_exc + hop, n_exc)

    barrier = pltpu.get_barrier_semaphore()
    has = (me_space > 0, me_space < n_space - 1)
    for side, peer in enumerate((left, right)):

        @pl.when(has[side])
        def _():
            pl.semaphore_signal(barrier, inc=1, device_id={"space": peer}, device_id_type=MESH)


    loads = []

    def load(src, dst):
        copy = pltpu.make_async_copy(src, dst, load_sem.at[len(loads)])
        copy.start()
        loads.append(copy)
        return copy

    def load_layers(src, dst):
        return [load(src.at[..., pl.ds(n * LAYER, LAYER)], dst.at[n]) for n in range(2)]

    got_nb = load(neighbor, nb_ref)
    got_e = load_layers(adj_e.at[0], e_ref)
    got_tb = load(table, tb_ref)
    got_h = load_layers(adj_h.at[0], h_ref)
    got_v = load_layers(inv_eps, v_ref)
    got_w = load_layers(drude, w_ref)
    got_j = load_layers(adj_j.at[0], j_ref)
    got_pe = load(ports, pe_ref)
    got_pp = load(profile.at[0], pp_ref)
    got_fb = load(face_table, fb_ref)
    got_f = load_layers(fwd_e.at[0], f_ref)
    got_dm = load(design, dm_ref)

    for hop in range(1, n_exc):
        peer = around(hop)
        pl.semaphore_signal(barrier, inc=1, device_id={"exc": peer}, device_id_type=MESH)

    sublane = lax.broadcasted_iota(jnp.int32, (8, LAYER), 0)
    lower = sublane < 4
    first_k = (sublane & 3) == 0
    last_k = (sublane & 3) == 3

    z_ref[...] = jnp.zeros(z_ref.shape, f32)
    for side in range(2):

        @pl.when(jnp.logical_not(has[side]))
        def _():
            for window in range(STEPS // 2):
                for kind in range(4):
                    recv_t[window, kind, side] = jnp.zeros((32, LAYER), f32)
            recv_v[side] = jnp.zeros((64, LAYER), f32)
            recv_nb[side] = jnp.zeros((6, LAYER), jnp.int32)


    got_nb.wait()
    table_nb = nb_ref[...]
    place = table_nb & (LAYER - 1)

    def face(number, layer):
        return place[number : number + 1, layer * LAYER : (layer + 1) * LAYER]

    def inside(number, layer):
        cut = table_nb[number : number + 1, layer * LAYER : (layer + 1) * LAYER]
        return (cut >= 0).astype(f32)

    edge_y = [jnp.where(lower, face(3, n), face(2, n)) for n in range(2)]
    edge_z = [jnp.where(first_k, face(5, n), face(4, n)) for n in range(2)]
    along_y = [jnp.concatenate([index] * 8, axis=0) for index in edge_y]
    low_z = [face(4, n) for n in range(2)]
    high_z = [face(5, n) for n in range(2)]
    between = [face(1, 0), face(0, 1)]
    beyond = [face(0, 0), face(1, 1)]
    exists = [inside(0, 0), inside(1, 1)]

    def product(field):
        high, low = halves(field)
        whole = jnp.dot(tb_ref[...], high, preferred_element_type=f32)
        rest = jnp.dot(tb_ref[0:192, :], low, preferred_element_type=f32)
        return whole[0:192] + (whole[192:384] + rest)

    calls = []

    def local_flux(field_ref):
        total = product(jnp.concatenate([field_ref[0], field_ref[1]], axis=1))
        zeros = jnp.zeros((48, LAYER), f32)
        slot = len(calls) % 2
        calls.append(slot)
        result = []
        for n in range(2):
            far = pick(field_ref[n, pl.ds(0, 32, stride=4), :], high_z[n])
            z_ref[slot, n, pl.ds(3, 32, stride=4), :] = jnp.concatenate(
                [far[16:32], -far[0:16]], axis=0
            )
            near = pick(field_ref[n, pl.ds(3, 32, stride=4), :], low_z[n])
            z_ref[slot, n, pl.ds(0, 32, stride=4), :] = jnp.concatenate(
                [-near[16:32], near[0:16]], axis=0
            )
            own = field_ref[n].reshape(3, 4, 2, 8, LAYER)
            edge = jnp.concatenate(
                [
                    jnp.where(lower, own[0, :, 0], own[0, :, 1]),
                    jnp.where(lower, own[2, :, 0], own[2, :, 1]),
                ],
                axis=0,
            )
            outer = pick(edge.reshape(64, LAYER), along_y[n]).reshape(8, 8, LAYER)
            outer = pltpu.roll(outer, 4, 1)
            zero = jnp.zeros((4, 8, LAYER), f32)
            o_x, o_z = outer[0:4], outer[4:8]
            to_x = jnp.stack([jnp.where(lower, o_z, zero), jnp.where(lower, zero, -o_z)], axis=1)
            to_z = jnp.stack([jnp.where(lower, -o_x, zero), jnp.where(lower, zero, o_x)], axis=1)
            if n == 0:
                side = turn(pick(rows_of(field_ref, 1, 0), between[0]), 1.0)
                to_y = jnp.concatenate([zeros, side[0:16]], axis=0)
                to_z2 = jnp.concatenate([zeros, side[16:32]], axis=0)
            else:
                side = turn(pick(rows_of(field_ref, 0, 48), between[1]), -1.0)
                to_y = jnp.concatenate([side[0:16], zeros], axis=0)
                to_z2 = jnp.concatenate([side[16:32], zeros], axis=0)
            extra = jnp.concatenate(
                [
                    z_ref[slot, n, 0:64] + to_x.reshape(64, LAYER),
                    z_ref[slot, n, 64:128] + to_y,
                    to_z.reshape(64, LAYER) + to_z2,
                ],
                axis=0,
            )
            result.append(total[:, n * LAYER : (n + 1) * LAYER] + extra)
        return result

    def from_y(rows, index):
        outer = pltpu.roll(pick(jnp.where(lower, rows[0:8], rows[8:16]), index), 4, 0)
        zero = jnp.zeros((8, LAYER), f32)
        return jnp.concatenate(
            [jnp.where(lower, outer, zero), jnp.where(lower, zero, -outer)], axis=0
        )

    def from_z(rows, index):
        parts_z = []
        zero = jnp.zeros((8, LAYER), f32)
        for half in (rows[0:8], rows[8:16]):
            outer = pick(half, index)
            parts_z.append(
                jnp.where(last_k, pltpu.roll(outer, 3, 0), zero)
                - jnp.where(first_k, pltpu.roll(outer, 5, 0), zero)
            )
        return jnp.concatenate(parts_z, axis=0)

    def remote(src, dst, sems, side):
        copy = pltpu.make_async_remote_copy(
            src_ref=src,
            dst_ref=dst,
            send_sem=sems[0],
            recv_sem=sems[1],
            device_id={"space": (left, right)[side]},
            device_id_type=MESH,
        )

        @pl.when(has[side])
        def _():
            copy.start()

        return copy, side

    def arrive(copies):
        for copy, side in copies:
            pl.when(has[1 - side])(copy.wait_recv)

    def leave(copies):
        for copy, side in copies:
            pl.when(has[side])(copy.wait_send)

    sent = []

    def keep_trace(window, kind, ref):
        for side in range(2):
            send_t[window, kind, side] = rows_of(ref, side, MINE[side])

    def send_trace(window, kind):
        copies = []
        for side in range(2):
            copies.append(
                remote(
                    send_t.at[window, kind, side],
                    recv_t.at[window, kind, 1 - side],
                    (send_sem.at[window, kind, side], recv_sem.at[window, kind, 1 - side]),
                    side,
                )
            )
        sent.extend(copies)
        return copies

    sens = [[jnp.zeros((64, LAYER), f32)] * 2 for _ in range(2)]

    def add(kind, n, field, weight):
        term = (field * weight).reshape(3, 64, LAYER)
        sens[kind][n] = sens[kind][n] + (term[0] + term[1] + term[2])

    def change_of(n, step):
        return f_ref[n, step + 1].astype(f32) - f_ref[n, step].astype(f32)

    def add_eps(step):
        for n in range(2):
            add(0, n, level_e[step, n], change_of(n, step))

    def add_drude(step):
        for n in range(2):
            add(1, n, level_j[step, n], f_ref[n, step].astype(f32))

    def drive(step):
        for n in range(2):
            electric = (level_e[step - 1, n] if step else e_ref[n]).reshape(3, 64, LAYER)
            current = level_j[step - 1, n] if step else j_ref[n]
            current = (1.0 - TIME_STEP * DAMPING) * current.reshape(3, 64, LAYER)
            current = current + w_ref[n] * electric
            level_j[step, n] = current.reshape(192, LAYER)
            push = v_ref[n] * (current + s_ref[n].reshape(3, 64, LAYER))
            e_ref[n] = (electric - push).reshape(192, LAYER)

    def gather_pixels(stacked):
        pixel = lax.broadcasted_iota(jnp.int32, (LAYER, 2 * LAYER), 0)
        members = ((dm_ref[...] & (LAYER - 1)) == pixel).astype(jnp.bfloat16)
        high, low = halves(stacked)
        contract = (((1,), (1,)), ((), ()))
        return lax.dot_general(
            members, high, contract, preferred_element_type=f32
        ) + lax.dot_general(members, low, contract, preferred_element_type=f32)

    def kick(n, flux):
        return (kick_ref[n] * flux.reshape(3, 64, LAYER)).reshape(192, LAYER)

    ghost_y, ghost_z = [None, None], [None, None]

    for copy in got_e:
        copy.wait()

    for window in range(STEPS // 2):
        step = 2 * window
        field = e_ref if window == 0 else level_e.at[step - 1]
        keep_trace(window, 0, field)
        if window > 0:
            e0 = send_trace(window, 0)
        if window == 0:
            got_tb.wait()
        flux = local_flux(field)
        if window == 0:
            for copy in got_h:
                copy.wait()
        for n in range(2):
            h_ref[n] = h_ref[n] + GAIN * flux[n]
        keep_trace(window, 1, h_ref)
        if window == 0:
            arrivals = has[0].astype(jnp.int32) + has[1].astype(jnp.int32)
            pl.semaphore_wait(barrier, arrivals + (n_exc - 1))
            e0 = send_trace(window, 0)
        h1 = send_trace(window, 1)
        if window == 0:
            once = []
            for side in range(2):
                lanes = pl.ds(side * LAYER, LAYER)
                for at, (src, dst) in enumerate(((inv_eps, recv_v), (neighbor, recv_nb))):
                    once.append(
                        remote(
                            src.at[:, lanes],
                            dst.at[1 - side],
                            (once_send_sem.at[at, side], once_recv_sem.at[at, 1 - side]),
                            side,
                        )
                    )

        if window == 0:
            for copy in got_w + got_v + got_j + [got_pe, got_pp]:
                copy.wait()
            element = lax.broadcasted_iota(jnp.int32, (2 * LAYER, LAYER), 0)
            chosen = ((pe_ref[...] & (2 * LAYER - 1)) == element).astype(jnp.bfloat16)
            high, low = halves(pp_ref[...])
            contract = (((1,), (1,)), ((), ()))
            source = lax.dot_general(
                high, chosen, contract, preferred_element_type=f32
            ) + lax.dot_general(low, chosen, contract, preferred_element_type=f32)
            for n in range(2):
                s_ref[n] = source[:, n * LAYER : (n + 1) * LAYER]
                kick_ref[n] = GAIN * v_ref[n]
                v_ref[n] = TIME_STEP * v_ref[n]
                w_ref[n] = TIME_STEP * w_ref[n]
        drive(step)
        flux = local_flux(h_ref)
        for n in range(2):
            e_ref[n] = e_ref[n] - kick(n, flux[n])
        keep_trace(window, 2, e_ref)
        e1 = send_trace(window, 2)
        flux = local_flux(e_ref)
        for n in range(2):
            h_ref[n] = h_ref[n] + GAIN * flux[n]
        keep_trace(window, 3, h_ref)
        h2 = send_trace(window, 3)

        if window == 0:
            for copy in got_f + [got_fb, got_dm]:
                copy.wait()
        add_drude(step)
        if step + 2 < STEPS:
            pass
        else:
            add_eps(step - 2)
            add_eps(step - 1)
            add_drude(step - 1)
            for n in range(2):
                for at in range(2):
                    change_ref[at, n] = change_of(n, step + at)
                late_ref[n] = f_ref[n, step + 1].astype(f32)
        arrive(e0)
        mine_dh, their_dh = [], []
        for side in range(2):
            sign = SIGN[side]
            outer = pick(recv_t[window, 0, side], beyond[side]) * exists[side]
            mine_dh.append(turn(outer, GAIN * sign))
            their_dh.append(turn(send_t[window, 0, side], -GAIN * sign))
        pairs = ((mine_dh[0], their_dh[1]), (mine_dh[1], their_dh[0]))
        spread = []
        for at in range(2):
            high, low = halves(jnp.concatenate(pairs[at], axis=1))
            spread.append(
                jnp.dot(
                    fb_ref[at],
                    jnp.concatenate([high, high, low], axis=0),
                    preferred_element_type=f32,
                )
            )

        def respond(side, ghost, across):
            layer = 2 + side if ghost else side
            start = THEIRS[side] if ghost else MINE[side]
            change = their_dh[side] if ghost else mine_dh[side]
            index_y = ghost_y[side] if ghost else edge_y[side]
            index_z = ghost_z[side] if ghost else edge_z[side]
            if ghost:
                out = spread[1 - side][:, LAYER : 2 * LAYER]
            else:
                out = spread[side][:, 0:LAYER]
            edge = from_y(change[16:32], index_y) + from_z(change[0:16], index_z)

            def with_face(rows, extra):
                end = start + 16
                middle = rows[start:end] + extra
                if start == 0:
                    return jnp.concatenate([middle, rows[end:64]], axis=0)
                return jnp.concatenate([rows[0:start], middle], axis=0)

            speed = kick_ref[layer]
            de_ref[layer, 0:64] = -speed * with_face(out[0:64], edge)
            de_ref[layer, 64:128] = -speed * with_face(out[64:128], across[0:16])
            de_ref[layer, 128:192] = -speed * with_face(out[128:192], across[16:32])

        def respond_ghosts():
            for side in range(2):
                across = send_t[window, 1, side] + mine_dh[side]
                respond(side, True, turn(across, -SIGN[side]))

        if window > 0:
            respond_ghosts()
        arrive(h1)
        for side in range(2):
            across = (pick(recv_t[window, 1, side], beyond[side]) + their_dh[side]) * exists[side]
            respond(side, False, turn(across, SIGN[side]))
        for n in range(2):
            level_e[step, n] = e_ref[n] + de_ref[n]
            add_rows(h_ref, n, MINE[n], mine_dh[n])
        flux = local_flux(de_ref)
        for n in range(2):
            h_ref[n] = h_ref[n] + GAIN * flux[n]

        if window == 0:
            arrive(once)
            for side in range(2):
                kick_ref[2 + side] = GAIN * pick(recv_v[side], beyond[side])
                far = recv_nb[side] & (LAYER - 1)
                back = jnp.broadcast_to(far[1 - side : 2 - side], (8, LAYER))

                def through(number):
                    rows = jnp.broadcast_to(far[number : number + 1], (8, LAYER))
                    return pick(back, pick(rows, beyond[side]))

                ghost_y[side] = jnp.where(lower, through(3), through(2))
                ghost_z[side] = jnp.where(first_k, through(5), through(4))
            respond_ghosts()

        def their_second():
            high, low = halves(jnp.concatenate([de_ref[2], de_ref[3]], axis=1))
            cuts = [tb_ref[at : at + 16, :] for at in (112, 176, 64, 128)]
            lows = [tb_ref[192 + at : 208 + at, :] for at in (112, 176, 64, 128)]
            whole = jnp.dot(jnp.concatenate(cuts + lows, axis=0), high, preferred_element_type=f32)
            rest = jnp.dot(jnp.concatenate(cuts, axis=0), low, preferred_element_type=f32)
            near = whole[0:64] + (whole[64:128] + rest)
            result = []
            for side in range(2):
                start = THEIRS[side]
                own = de_ref[2 + side, start : start + 16]
                edge = jnp.concatenate(
                    [-from_z(own, ghost_z[side]), -from_y(own, ghost_y[side])], axis=0
                )
                across = turn(rows_of(level_e.at[step], side, MINE[side]), -SIGN[side])
                lanes = slice(side * LAYER, (side + 1) * LAYER)
                at = slice(32 * side, 32 * side + 32)
                result.append(their_dh[side] + GAIN * (near[at, lanes] + edge + across))
            return result

        arrive(e1)
        for side in range(2):
            outer = pick(recv_t[window, 2, side], beyond[side])
            outer = (outer + rows_of(de_ref, 2 + side, THEIRS[side])) * exists[side]
            add_rows(h_ref, side, MINE[side], turn(outer, GAIN * SIGN[side]))
        if step + 2 == STEPS:
            stores = []
            for n in range(2):
                lanes = pl.ds(n * LAYER, LAYER)
                copy = pltpu.make_async_copy(h_ref.at[n], out_h.at[0, :, lanes], store_sem.at[n])
                copy.start()
                stores.append(copy)

        drive(step + 1)
        flux = local_flux(h_ref)
        for n in range(2):
            level_e[step + 1, n] = e_ref[n] - kick(n, flux[n])
        if step + 2 == STEPS:
            for n in range(2):
                add(0, n, level_e[step, n], change_ref[0, n])
                add(1, n, level_j[step + 1, n], late_ref[n])
            sums[...] = gather_pixels(
                jnp.concatenate(
                    [jnp.concatenate(sens[0], axis=1), jnp.concatenate(sens[1], axis=1)], axis=0
                )
            )
        their_dh2 = their_second()
        arrive(h2)
        for side in range(2):
            outer = pick(recv_t[window, 3, side], beyond[side])
            outer = turn((outer + their_dh2[side]) * exists[side], -SIGN[side])
            speed = kick_ref[side, MINE[side] : MINE[side] + 16]
            add_rows(
                level_e.at[step + 1],
                side,
                MINE[side],
                jnp.concatenate([speed * outer[0:16], speed * outer[16:32]], axis=0),
            )

    for n in range(2):
        lanes = pl.ds(n * LAYER, LAYER)
        copy = pltpu.make_async_copy(
            level_e.at[STEPS - 1, n], out_e.at[0, :, lanes], store_sem.at[2 + n]
        )
        copy.start()
        stores.append(copy)
    sens[0] = [jnp.zeros((64, LAYER), f32)] * 2
    for n in range(2):
        add(0, n, level_e[STEPS - 1, n], change_ref[1, n])
    sums[:, 0:64] += gather_pixels(jnp.concatenate(sens[0], axis=1))
    part_copies = {}
    for hop in FAR_FIRST if n_exc == 16 else range(1, n_exc):
        peer = around(hop)
        start = pl.multiple_of(peer * own_rows, own_rows)
        copy = pltpu.make_async_remote_copy(
            src_ref=sums.at[pl.ds(start, own_rows)],
            dst_ref=parts.at[hop],
            send_sem=part_send_sem.at[hop],
            recv_sem=part_recv_sem.at[hop],
            device_id={"exc": peer},
            device_id_type=MESH,
        )
        copy.start()
        part_copies[hop] = copy
    leave(sent + once)
    total = sums[pl.ds(pl.multiple_of(me_exc * own_rows, own_rows), own_rows)]
    for hop in range(1, n_exc):
        part_copies[hop].wait_recv()
        total = total + parts[hop]
    total = total * (1.0 / n_exc)
    out_eps[...] = total[:, 0:64]
    out_drude[...] = total[:, 64:128]
    for copy in part_copies.values():
        copy.wait_send()
    for copy in stores:
        copy.wait()


def write_kernel(e_in, h_in, a_in, b_in, e_out, h_out, a_out, b_out, sem):
    copies = [
        pltpu.make_async_copy(src, dst, sem.at[at])
        for at, (src, dst) in enumerate(
            ((e_in, e_out), (h_in, h_out), (a_in, a_out), (b_in, b_out))
        )
    ]
    for copy in copies:
        copy.start()
    for copy in copies:
        copy.wait()


def write(*arrays):
    spec = pl.BlockSpec(memory_space=pltpu.HBM)
    return pl.pallas_call(
        write_kernel,
        out_shape=tuple(jax.ShapeDtypeStruct(a.shape, a.dtype) for a in arrays),
        in_specs=[pl.BlockSpec(memory_space=pltpu.VMEM)] * 4,
        out_specs=(spec,) * 4,
        scratch_shapes=[pltpu.SemaphoreType.DMA((4,))],
        compiler_params=pltpu.CompilerParams(vmem_limit_bytes=2 << 20),
        name="write_out",
    )(*arrays)


def local(n_exc, n_space, *args):
    (adj_e, adj_h, adj_j, fwd_e, inv_eps, drude, neighbor, design, ports, profile) = args
    own_rows = LAYER // n_exc
    f32 = jnp.float32
    anywhere = pl.BlockSpec(memory_space=pltpu.HBM)
    in_vmem = pl.BlockSpec(memory_space=pltpu.VMEM)
    new_e, new_h, grad_eps, grad_drude = pl.pallas_call(
        functools.partial(kernel, n_exc, n_space),
        out_shape=(
            jax.ShapeDtypeStruct(adj_e.shape, f32),
            jax.ShapeDtypeStruct(adj_h.shape, f32),
            jax.ShapeDtypeStruct((own_rows, 64), f32),
            jax.ShapeDtypeStruct((own_rows, 64), f32),
        ),
        in_specs=[anywhere] * 12,
        out_specs=(anywhere, anywhere, in_vmem, in_vmem),
        scratch_shapes=[
            pltpu.VMEM((2, 192, LAYER), f32),
            pltpu.VMEM((2, 192, LAYER), f32),
            pltpu.VMEM((2, 192, LAYER), f32),
            pltpu.VMEM((STEPS, 2, 192, LAYER), f32),
            pltpu.VMEM((STEPS, 2, 192, LAYER), f32),
            pltpu.VMEM((2, 2, 192, LAYER), f32),
            pltpu.VMEM((2, 192, LAYER), f32),
            pltpu.VMEM((2, 192, LAYER), f32),
            pltpu.VMEM((2, 2, LAYER, LAYER), f32),
            pltpu.VMEM((4, 192, LAYER), f32),
            pltpu.VMEM((2, STEPS + 1, 192, LAYER), jnp.bfloat16),
            pltpu.VMEM((2, 64, LAYER), f32),
            pltpu.VMEM((2, 64, LAYER), f32),
            pltpu.VMEM((4, 64, LAYER), f32),
            pltpu.VMEM((6, 2 * LAYER), jnp.int32),
            pltpu.VMEM((1, 2 * LAYER), jnp.int32),
            pltpu.VMEM((1, LAYER), jnp.int32),
            pltpu.VMEM((192, LAYER), f32),
            pltpu.VMEM((384, 192), jnp.bfloat16),
            pltpu.VMEM((2, 192, 96), jnp.bfloat16),
            pltpu.VMEM((STEPS // 2, 4, 2, 32, LAYER), f32),
            pltpu.VMEM((STEPS // 2, 4, 2, 32, LAYER), f32),
            pltpu.VMEM((2, 64, LAYER), f32),
            pltpu.VMEM((2, 6, LAYER), jnp.int32),
            pltpu.VMEM((LAYER, LAYER), f32),
            pltpu.VMEM((n_exc, own_rows, LAYER), f32),
            pltpu.SemaphoreType.DMA((24,)),
            pltpu.SemaphoreType.DMA((STEPS // 2, 4, 2)),
            pltpu.SemaphoreType.DMA((STEPS // 2, 4, 2)),
            pltpu.SemaphoreType.DMA((2, 2)),
            pltpu.SemaphoreType.DMA((2, 2)),
            pltpu.SemaphoreType.DMA((n_exc,)),
            pltpu.SemaphoreType.DMA((n_exc,)),
            pltpu.SemaphoreType.DMA((4,)),
        ],
        compiler_params=pltpu.CompilerParams(
            collective_id=0, has_side_effects=True, vmem_limit_bytes=16 << 20
        ),
        name="adjoint_steps",
    )(
        *[pltpu.with_memory_space_constraint(x, pltpu.HBM) for x in (adj_e, adj_h, adj_j, fwd_e, inv_eps, drude, neighbor, design.reshape(1, 2 * LAYER), ports, profile, jnp.asarray(split_table()), jnp.asarray(split_faces()))]
    )
    new_e, new_h, grad_eps, grad_drude = write(new_e, new_h, grad_eps, grad_drude)
    return new_e, new_h, grad_eps.T, grad_drude.T


def solution(mesh):
    return jax.shard_map(
        functools.partial(local, mesh.shape["exc"], mesh.shape["space"]),
        mesh=mesh,
        in_specs=(
            P("exc", None, "space"),
            P("exc", None, "space"),
            P("exc", None, "space"),
            P("exc", None, None, "space"),
            P(None, "space"),
            P(None, "space"),
            P(None, "space"),
            P("space"),
            P("exc", "space"),
            P("exc", None, "space"),
        ),
        out_specs=(
            P("exc", None, "space"),
            P("exc", None, "space"),
            P(None, ("space", "exc")),
            P(None, ("space", "exc")),
        ),
        check_vma=False,
    )
```
